256 devices in a mesh: row: 16 (over y, x), col: 16 (over z, core).
Axes of the slice: x: 4, y: 4, z: 8, core: 2. Of those that a mesh axis runs over, the one named last changes fastest.
Arguments:
- trailing: float32 [8192, 8192], P('row', 'col'), may hold values from -6 to 6
- panel_block: float32 [8192, 512], P('row'), may hold values from -1 to 1
Outputs:
- updated: float32 [8192, 8192], P('row', 'col')
- band_block: float32 [512, 512], replicated
The draws below stay inside these ranges and needn't reach their ends.
All inputs are finite; a program needn't handle non-finite values.
Results may differ from the reference program's by a relative error of at most 0.00015.
Values sent between devices are 32-bit elements; how exact they have to be, the bound alone decides.
A program may use at most 64 MiB of HBM per device.

```python
import math
import jax
import jax.numpy as jnp
from jax import lax

BAND = 512
ORDER = 8192


def draw_trailing(key, part):
    key_values = jax.random.fold_in(jax.random.fold_in(key, 11), 0)
    values = jax.random.truncated_normal(key_values, -4.0, 4.0, (ORDER, ORDER), jnp.float32)
    return 0.5 * (values + values.T)


def draw_panel_block(key, part):
    key_values, key_rows, key_cols = jax.random.split(jax.random.fold_in(key, 23), 3)
    col_scale = jnp.exp(jax.random.uniform(key_cols, (BAND,), jnp.float32, -math.log(10.0), 0.0))
    values = jax.random.truncated_normal(key_values, -3.0, 3.0, (ORDER, BAND), jnp.float32)
    row_scale = jnp.exp(jax.random.uniform(key_rows, (ORDER,), jnp.float32, -math.log(10.0), 0.0))
    factor = min(4.0 / math.sqrt(ORDER), 0.25)
    return values * row_scale[:, None] * col_scale[None, :] * factor


def setup_inputs(seed: int = 0) -> dict:
    seeds = jax.random.split(jax.random.key(seed), 3)
    trailing = draw_trailing(jax.random.fold_in(seeds[2], 71), 0)
    panel_block = draw_panel_block(jax.random.fold_in(seeds[2], 71), 0)
    return {"trailing": trailing, "panel_block": panel_block}


PRECISE = lax.Precision.HIGHEST

def product(former, latter):
    return jnp.dot(former.astype(jnp.float32), latter.astype(jnp.float32), precision=PRECISE, preferred_element_type=jnp.float32)

def reference(trailing, panel_block):
    identity = jnp.eye(BAND, dtype=jnp.float32)
    gram = product(panel_block.T, panel_block)
    lower_factor = jnp.linalg.cholesky(gram)
    orthonormal = jax.scipy.linalg.solve_triangular(lower_factor, panel_block.T, lower=True).T
    inverse = jnp.linalg.solve(identity + orthonormal[:BAND].T, identity)
    reflector = orthonormal.at[:BAND].add(identity)
    applied = product(trailing, product(reflector, inverse))
    coupling = product(inverse.T, product(reflector.T, applied))
    correction = applied - 0.5 * product(reflector, coupling)
    left_side = jnp.concatenate([reflector, correction], axis=1)
    right_side = jnp.concatenate([correction, reflector], axis=1)
    updated = trailing - product(left_side, right_side.T)
    return (updated, -lower_factor.T)
```

```python
import functools
import jax
import jax.numpy as jnp
from jax import lax
from jax.experimental import pallas as pl
from jax.experimental.pallas import tpu as pltpu
from jax.sharding import PartitionSpec as P

HI = lax.Precision.HIGHEST
F32 = jnp.float32
BF16 = jnp.bfloat16
MESH = pl.DeviceIdType.MESH
G, P0, B0, F0, R = range(5)


def dotg(a, b, ca, cb):
    return lax.dot_general(
        a, b, (((ca,), (cb,)), ((), ())), precision=HI, preferred_element_type=F32
    )


def split(x):
    high = x.astype(BF16)
    return high, (x - high.astype(F32)).astype(BF16)


def dot3(a, b, ca, cb):
    ah, al = a if isinstance(a, tuple) else split(a)
    bh, bl = b if isinstance(b, tuple) else split(b)
    dims = (((ca,), (cb,)), ((), ()))
    d = functools.partial(lax.dot_general, dimension_numbers=dims, preferred_element_type=F32)
    return d(ah, bh) + (d(ah, bl) + d(al, bh))


def bc(x):
    return jnp.broadcast_to(x, (8, 128))


def leaf(d):
    sub = lax.broadcasted_iota(jnp.int32, (8, 128), 0)
    lane = lax.broadcasted_iota(jnp.int32, (8, 128), 1)
    d = list(d)
    inv = [(lane == sub + 8 * q).astype(F32) for q in range(16)]
    upper, lower_inv = [], []
    for q in range(16):
        cb = [bc(d[q][:, 8 * q + j : 8 * q + j + 1]) for j in range(8)]
        mul = [[bc(d[p][:, 8 * q + j : 8 * q + j + 1]) for j in range(8)] for p in range(q + 1, 16)]
        zd, zi = d[q], inv[q]
        ud = jnp.zeros((8, 128), F32)
        ui = ud
        for j in range(8):
            pivot = bc(cb[j][j : j + 1, :])
            r = 1.0 / pivot
            rs = lax.rsqrt(pivot)
            rd, ri = bc(zd[j : j + 1, :]), bc(zi[j : j + 1, :])
            mine = sub == j
            ud, ui = jnp.where(mine, rd * rs, ud), jnp.where(mine, ri * rs, ui)
            pd, pi = rd * r, ri * r
            zd = jnp.where(mine, pd, zd - cb[j] * pd)
            zi = jnp.where(mine, pi, zi - cb[j] * pi)
            for k in range(j + 1, 8):
                t = bc(cb[k][j : j + 1, :]) * r
                cb[k] = jnp.where(mine, t, cb[k] - cb[j] * t)
        upper.append(jnp.where(lane >= sub + 8 * q, ud, 0.0))
        lower_inv.append(ui)
        zds = [bc(zd[j : j + 1, :]) for j in range(8)]
        zis = [bc(zi[j : j + 1, :]) for j in range(8)]
        for p in range(q + 1, 16):
            m = mul[p - q - 1]
            x, y = d[p], inv[p]
            for j in range(8):
                x, y = x - m[j] * zds[j], y - m[j] * zis[j]
            d[p], inv[p] = x, y
    return upper, lower_inv


def factor_block(b, w, u, li):
    s, e = 128 * b, 128 * b + 128
    upper, lower_inv = leaf([w[s + 8 * q : s + 8 * q + 8, s:e] for q in range(16)])
    for q in range(16):
        u[s + 8 * q : s + 8 * q + 8, s:e] = upper[q]
        li[s + 8 * q : s + 8 * q + 8, s:e] = lower_inv[q]
    lb = li[s:e, s:e]
    if b < 3:
        u[s:e, e:] = dotg(lb, w[s:e, e:], 1, 0)
    if b > 0:
        li[s:e, :s] = dotg(lb, li[s:e, :s], 1, 0)
    if b < 3:
        ut = u[s:e, e:]
        w[e:, e:] -= dotg(ut, ut, 0, 0)
        li[e:, :e] -= dotg(ut, li[s:e, :e], 0, 0)


def factor_kernel(g, nu, li, w, u):
    w[...] = g[...].reshape(512, 512)
    u[...] = jnp.zeros((512, 512), F32)
    li[...] = jnp.zeros((512, 512), F32)
    for b in range(4):
        factor_block(b, w, u, li)
    nu[...] = -u[...]


def comm_kernel(
    n, a, p, cm, pc, bct, a0c, br, fr,
    gp, bp, grs, brs, rp, rrs, bq, bsw, bsum, bz, send, recv,
):
    hs, zc = 256 // n, n // 2
    zs, ps = 256 // zc, 128 // n
    r, c = lax.axis_index("row"), lax.axis_index("col")
    z, k = lax.div(c, 2), lax.rem(c, 2)
    partner = c + 1 - 2 * k
    sent = []

    def at(i, size):
        return pl.ds(pl.multiple_of(i * size, size), size)

    def copy(src, dst, s, axis, index):
        return pltpu.make_async_remote_copy(
            src_ref=src, dst_ref=dst, send_sem=send.at[s], recv_sem=recv.at[s],
            device_id={axis: index}, device_id_type=MESH,
        )

    def wait(ref, s, sems=recv):
        pltpu.make_async_copy(ref, ref, sems.at[s]).wait()

    rows = [lax.rem(r + j, n) for j in range(1, n)]
    cols = [lax.rem(c + j, n) for j in range(1, n)]
    cores = [lax.rem(c + 2 * j, n) for j in range(1, zc)]

    barrier = pltpu.get_barrier_semaphore()
    for i in rows:
        pl.semaphore_signal(barrier, inc=1, device_id={"row": i}, device_id_type=MESH)
    for i in cols:
        pl.semaphore_signal(barrier, inc=1, device_id={"col": i}, device_id_type=MESH)
    pl.semaphore_wait(barrier, 2 * n - 2)

    PC_S, A0_S, P0_S, FR_S, G_RS, B_RS, PC_AG, A0_AG, BC_AG, CM_AG = range(10)
    CM_SW, B0_S, F0_S, R_RS, R_B, BQ_SW, B_Z, BR_AG, BR_SW, FR_AG, FR_SW = (
        15, 20, 21, 22, 23, 24, 25, 26, 27, 28, 29)
    own, own_z = at(r, hs), at(z, zs)

    @pl.when(r == c)
    def _():
        for i in rows:
            copy(p.at[:, at(i, hs)], pc.at[:, at(i, hs)], PC_S, "row", i).start()
        pc[:, own] = p[:, own]

    @pl.when(r == 0)
    def _():
        for i in rows:
            copy(p.at[k, at(i, hs)], cm.at[P0, k, at(i, hs)], P0_S, "row", i).start()
            copy(a.at[:, at(i, hs)], a0c.at[:, at(i, hs)], A0_S, "row", i).start()
        cm[P0, k, own] = p[k, own]
        a0c[:, own] = a[:, own]

    @pl.when(c == 0)
    def _():
        for j in cols:
            kk, zz = lax.rem(j, 2), lax.div(j, 2)
            copy(a.at[kk, at(zz, zs)], fr.at[kk, at(zz, zs)], FR_S, "col", j).start()
        fr[k, own_z] = a[k, own_z]

    panel = p[...].reshape(512, 512)
    half = pl.ds(pl.multiple_of(k * 256, 256), 256)
    gp[...] = dotg(jnp.concatenate([p[0, :, half], p[1, :, half]], axis=0), panel, 0, 0)
    for i in rows:
        copy(gp.at[at(i, hs)], grs.at[r], G_RS, "row", i).start()
    grs[r] = gp[own]
    bp[...] = dot3(panel, a[...].reshape(512, 512), 0, 0).reshape(2, 256, 512)
    for i in rows:
        copy(bp.at[:, at(i, hs)], brs.at[r], B_RS, "row", i).start()
    brs[r] = bp[:, own]

    @pl.when(r != 0)
    def _():
        wait(cm.at[P0, k, own], P0_S)
        wait(a0c.at[:, own], A0_S)

    for i in rows:
        copy(cm.at[P0, k, own], cm.at[P0, k, own], CM_AG + P0, "row", i).start()

    wait(grs.at[pl.ds(0, n - 1)], G_RS)
    cm[G, k, own] = jnp.sum(grs[...], axis=0)
    for i in rows:
        copy(cm.at[G, k, own], cm.at[G, k, own], CM_AG + G, "row", i).start()

    @pl.when(r != c)
    def _():
        wait(pc.at[:, own], PC_S)

    for i in rows:
        copy(pc.at[:, own], pc.at[:, own], PC_AG, "row", i).start()

    @pl.when(c != 0)
    def _():
        wait(fr.at[k, own_z], FR_S)

    for j in cores:
        copy(fr.at[k, own_z], fr.at[k, own_z], FR_AG, "col", j).start()

    wait(brs.at[pl.ds(0, n - 1)], B_RS)
    bct[:, own] = jnp.sum(brs[...], axis=0)
    for i in rows:
        copy(bct.at[:, own], bct.at[:, own], BC_AG, "row", i).start()

    @pl.when(c == 0)
    def _():
        for j in cols:
            kk = lax.rem(j, 2)
            copy(bct.at[kk, own], cm.at[B0, kk, own], B0_S, "col", j).start()
            copy(a0c.at[kk, own], cm.at[F0, kk, own], F0_S, "col", j).start()
        cm[B0, k, own] = bct[k, own]
        cm[F0, k, own] = a0c[k, own]

    for i in rows:
        copy(a0c.at[:, own], a0c.at[:, own], A0_AG, "row", i).start()

    def gathered(item):
        wait(cm.at[item, k, pl.ds(0, 256 - hs)], CM_AG + item)
        copy(cm.at[item, k], cm.at[item, k], CM_SW + item, "col", partner).start()

    gathered(G)
    gathered(P0)

    wait(pc.at[:, pl.ds(0, 256 - hs)], PC_AG)
    pcw = split(pc[...].reshape(512, 512))
    rp[...] = dot3(bct[:, own].reshape(2 * hs, 512), pcw, 1, 0).reshape(4, ps, 512)
    where = [(h + 2 * q * max(1, zc // 4), 2 * h + q, h, q) for h in range(2) for q in range(2)]
    for dst, piece, h, q in where:
        @pl.when(c != dst)
        def _():
            copy(rp.at[piece], rrs.at[c], R_RS, "col", dst).start()

        @pl.when(c == dst)
        def _():
            rrs[c] = rp[piece]

    bq[...] = dot3(a[...].reshape(512, 512), pcw, 1, 0).reshape(2, 256, 512)
    copy(bq.at[1 - k], bsw, BQ_SW, "col", partner).start()

    @pl.when(c != 0)
    def _():
        wait(cm.at[B0, k, own], B0_S)
        wait(cm.at[F0, k, own], F0_S)

    for i in rows:
        copy(cm.at[B0, k, own], cm.at[B0, k, own], CM_AG + B0, "row", i).start()
    for i in rows:
        copy(cm.at[F0, k, own], cm.at[F0, k, own], CM_AG + F0, "row", i).start()

    for dst, piece, h, q in where:
        @pl.when(c == dst)
        def _():
            wait(rrs.at[pl.ds(0, n - 1)], R_RS)
            sl = pl.ds(pl.multiple_of(r * hs + q * ps, ps), ps)
            cm[R, h, sl] = jnp.sum(rrs[...], axis=0)
            for j in cores:
                copy(cm.at[R, h, sl], cm.at[R, h, sl], R_B, "col", j).start()

    wait(bsw, BQ_SW)
    bsum[...] = bq[k] + bsw[...]
    for j in cores:
        copy(bsum.at[at(lax.div(j, 2), zs)], bz.at[z], B_Z, "col", j).start()
    bz[z] = bsum[own_z]

    reducer = functools.reduce(jnp.logical_or, [c == dst for dst, *_ in where])

    @pl.when(reducer)
    def _():
        wait(rrs.at[0], R_B)

    @pl.when(jnp.logical_not(reducer))
    def _():
        wait(rrs.at[pl.ds(0, 2)], R_B)

    for i in rows:
        copy(cm.at[R, k, own], cm.at[R, k, own], CM_AG + R, "row", i).start()

    wait(fr.at[k, pl.ds(0, 256 - zs)], FR_AG)
    copy(fr.at[k], fr.at[k], FR_SW, "col", partner).start()

    wait(bz.at[pl.ds(0, zc - 1)], B_Z)
    br[k, own_z] = jnp.sum(bz[...], axis=0)
    for j in cores:
        copy(br.at[k, own_z], br.at[k, own_z], BR_AG, "col", j).start()

    gathered(B0)
    gathered(F0)
    gathered(R)
    wait(br.at[k, pl.ds(0, 256 - zs)], BR_AG)
    copy(br.at[k], br.at[k], BR_SW, "col", partner).start()

    wait(bct.at[:, pl.ds(0, 256 - hs)], BC_AG)
    wait(a0c.at[:, pl.ds(0, 256 - hs)], A0_AG)
    for item in range(5):
        wait(cm.at[item, 1 - k], CM_SW + item)
    wait(fr.at[1 - k], FR_SW)
    wait(br.at[1 - k], BR_SW)

    big, small = pc.at[:, pl.ds(0, 256 - hs)], bsw.at[pl.ds(0, 256 - hs)]
    zbig = bsw.at[pl.ds(0, 256 - zs)]

    @pl.when(r == c)
    def _():
        wait(big, PC_S, send)

    @pl.when(r == 0)
    def _():
        wait(small, P0_S, send)
        wait(big, A0_S, send)

    @pl.when(c == 0)
    def _():
        wait(fr.at[:, pl.ds(0, 256 - zs // 2)], FR_S, send)
        wait(small, B0_S, send)
        wait(small, F0_S, send)

    for s in (B_RS, PC_AG, A0_AG, BC_AG):
        wait(big, s, send)
    for s in (G_RS, CM_AG, CM_AG + 1, CM_AG + 2, CM_AG + 3, CM_AG + 4):
        wait(small, s, send)
    for s in (CM_SW, CM_SW + 1, CM_SW + 2, CM_SW + 3, CM_SW + 4, BQ_SW, BR_SW, FR_SW):
        wait(bsw, s, send)
    for s in (B_Z, BR_AG, FR_AG):
        wait(zbig, s, send)

    @pl.when(reducer)
    def _():
        wait(rrs.at[pl.ds(0, 3)], R_RS, send)
        wait(rrs.at[pl.ds(0, zc - 1)], R_B, send)

    @pl.when(jnp.logical_not(reducer))
    def _():
        wait(rrs.at[pl.ds(0, 4)], R_RS, send)


def final_kernel(a, p, cm, pc, bct, a0c, br, fr, li, out, x, e, s, yt):
    r, c = lax.axis_index("row"), lax.axis_index("col")

    def whole(ref):
        return ref[...].reshape(512, 512)

    eye = (
        lax.broadcasted_iota(jnp.int32, (512, 512), 0)
        == lax.broadcasted_iota(jnp.int32, (512, 512), 1)
    ).astype(F32)
    lis = split(li[...])
    start = 0.9
    m = eye + dot3(lis, cm[P0].reshape(512, 512), 1, 1)
    e[...] = eye - start * m
    x[...] = start * (eye + e[...])

    def size(value):
        return jnp.sum(value * value)

    def more(state):
        step, now = state
        return jnp.logical_and(step < 48, now > 1e-3)

    def square(state):
        step, _ = state
        es = split(e[...])
        ee = dot3(es, es, 1, 0)
        e[...] = ee
        x[...] += dot3(x[...], ee, 1, 0)
        return step + 1, size(ee)

    lax.while_loop(more, square, (jnp.int32(0), jnp.float32(1.0)))
    xs = split(x[...])
    rest = eye - dot3(m, xs, 1, 0)
    inv = x[...] + dot3(xs, rest, 1, 0)
    nis = split(dot3(inv, lis, 1, 0))

    kt = dot3(lis, cm[B0].reshape(512, 512), 1, 0)
    s[...] = (
        dot3(lis, dot3(cm[R].reshape(512, 512), lis, 1, 1), 1, 0)
        + kt + kt.T + cm[F0].reshape(512, 512)
    )
    yt[...] = jnp.where(c == 0, eye, dot3(nis, whole(pc), 1, 1))
    yts = split(yt[...])
    zt = dot3(lis, whole(bct), 1, 0) + whole(a0c) - dot3(s[...], yts, 1, 0)
    y = jnp.where(r == 0, eye, dot3(whole(p), nis, 1, 1))
    u = dot3(whole(br), lis, 1, 1) + whole(fr)
    out[...] = whole(a) - dot3(y, zt, 1, 0) - dot3(u, yts, 1, 0)


def solution(mesh):
    n = mesh.shape["row"]
    hs, zc = 256 // n, n // 2
    zs, ps = 256 // zc, 128 // n
    vm = pl.BlockSpec(memory_space=pltpu.VMEM)
    sq = jax.ShapeDtypeStruct((512, 512), F32)
    two = jax.ShapeDtypeStruct((2, 256, 512), F32)

    def step(trailing, panel):
        a, p = trailing.reshape(2, 256, 512), panel.reshape(2, 256, 512)
        cm, pc, bct, a0c, br, fr = pl.pallas_call(
            functools.partial(comm_kernel, n),
            out_shape=[jax.ShapeDtypeStruct((5, 2, 256, 512), F32)] + [two] * 5,
            in_specs=[vm] * 2,
            out_specs=[vm] * 6,
            scratch_shapes=[
                pltpu.VMEM((256, 512), F32),
                pltpu.VMEM((2, 256, 512), F32),
                pltpu.VMEM((n, hs, 512), F32),
                pltpu.VMEM((n, 2, hs, 512), F32),
                pltpu.VMEM((4, ps, 512), F32),
                pltpu.VMEM((n, ps, 512), F32),
                pltpu.VMEM((2, 256, 512), F32),
                pltpu.VMEM((256, 512), F32),
                pltpu.VMEM((256, 512), F32),
                pltpu.VMEM((zc, zs, 512), F32),
                pltpu.SemaphoreType.DMA((32,)),
                pltpu.SemaphoreType.DMA((32,)),
            ],
            compiler_params=pltpu.CompilerParams(collective_id=0, has_side_effects=True),
            name="exchange",
        )(a, p)
        nu, li = pl.pallas_call(
            factor_kernel,
            out_shape=[sq, sq],
            in_specs=[vm],
            out_specs=[vm] * 2,
            scratch_shapes=[pltpu.VMEM((512, 512), F32)] * 2,
            name="factor",
        )(cm[G])
        out = pl.pallas_call(
            final_kernel,
            out_shape=sq,
            in_specs=[vm] * 9,
            out_specs=vm,
            scratch_shapes=[pltpu.VMEM((512, 512), F32)] * 4,
            name="update",
        )(a, p, cm, pc, bct, a0c, br, fr, li)
        return out, nu

    return jax.shard_map(
        step, mesh=mesh, in_specs=(P("row", "col"), P("row", None)),
        out_specs=(P("row", "col"), P()), check_vma=False,
    )
```

```python
import functools
import jax
import jax.numpy as jnp
from jax import lax
from jax.experimental import pallas as pl
from jax.experimental.pallas import tpu as pltpu
from jax.sharding import PartitionSpec as P

HI = lax.Precision.HIGHEST
F32 = jnp.float32
BF16 = jnp.bfloat16
MESH = pl.DeviceIdType.MESH
G, P0, B0, F0, R = range(5)


def dotg(a, b, ca, cb):
    return lax.dot_general(
        a, b, (((ca,), (cb,)), ((), ())), precision=HI, preferred_element_type=F32
    )


def split(x):
    high = x.astype(BF16)
    return high, (x - high.astype(F32)).astype(BF16)


def dot3(a, b, ca, cb):
    ah, al = a if isinstance(a, tuple) else split(a)
    bh, bl = b if isinstance(b, tuple) else split(b)
    dims = (((ca,), (cb,)), ((), ()))
    d = functools.partial(lax.dot_general, dimension_numbers=dims, preferred_element_type=F32)
    return d(ah, bh) + (d(ah, bl) + d(al, bh))


def bc(x):
    return jnp.broadcast_to(x, (8, 128))


def leaf(d, pause):
    sub = lax.broadcasted_iota(jnp.int32, (8, 128), 0)
    lane = lax.broadcasted_iota(jnp.int32, (8, 128), 1)
    d = list(d)
    inv = [(lane == sub + 8 * q).astype(F32) for q in range(16)]
    upper, lower_inv = [], []
    for q in range(16):
        cb = [bc(d[q][:, 8 * q + j : 8 * q + j + 1]) for j in range(8)]
        mul = [[bc(d[p][:, 8 * q + j : 8 * q + j + 1]) for j in range(8)] for p in range(q + 1, 16)]
        zd, zi = d[q], inv[q]
        ud = jnp.zeros((8, 128), F32)
        ui = ud
        for j in range(8):
            pivot = bc(cb[j][j : j + 1, :])
            r = 1.0 / pivot
            rs = lax.rsqrt(pivot)
            rd, ri = bc(zd[j : j + 1, :]), bc(zi[j : j + 1, :])
            mine = sub == j
            ud, ui = jnp.where(mine, rd * rs, ud), jnp.where(mine, ri * rs, ui)
            pd, pi = rd * r, ri * r
            zd = jnp.where(mine, pd, zd - cb[j] * pd)
            zi = jnp.where(mine, pi, zi - cb[j] * pi)
            for k in range(j + 1, 8):
                t = bc(cb[k][j : j + 1, :]) * r
                cb[k] = jnp.where(mine, t, cb[k] - cb[j] * t)
        upper.append(jnp.where(lane >= sub + 8 * q, ud, 0.0))
        lower_inv.append(ui)
        zds = [bc(zd[j : j + 1, :]) for j in range(8)]
        zis = [bc(zi[j : j + 1, :]) for j in range(8)]
        for p in range(q + 1, 16):
            m = mul[p - q - 1]
            x, y = d[p], inv[p]
            for j in range(8):
                x, y = x - m[j] * zds[j], y - m[j] * zis[j]
            d[p], inv[p] = x, y
        if q in (3, 7, 11):
            pause()
    return upper, lower_inv


def factor_block(b, w, u, li, pause):
    s, e = 128 * b, 128 * b + 128
    upper, lower_inv = leaf([w[s + 8 * q : s + 8 * q + 8, s:e] for q in range(16)], pause)
    for q in range(16):
        u[s + 8 * q : s + 8 * q + 8, s:e] = upper[q]
        li[s + 8 * q : s + 8 * q + 8, s:e] = lower_inv[q]
    lb = li[s:e, s:e]
    if b < 3:
        u[s:e, e:] = dotg(lb, w[s:e, e:], 1, 0)
    if b > 0:
        li[s:e, :s] = dotg(lb, li[s:e, :s], 1, 0)
    if b < 3:
        ut = u[s:e, e:]
        w[e:, e:] -= dotg(ut, ut, 0, 0)
        li[e:, :e] -= dotg(ut, li[s:e, :e], 0, 0)


NAMES = ["pc_s", "p0_s", "a0_s", "fr_s", "g_rs", "b0_s", "f0_s", "r_rs"]
NAMES += ["r_b", "bq_w", "bz", "br_g", "br_w", "fr_g", "fr_w"]
NAMES += [(item, step) for item in ("pc", "bc", "a0", "rs") for step in range(4)]
NAMES += [(item, step) for item in range(5) for step in range(5)]
SEM = {name: i for i, name in enumerate(NAMES)}


def main_kernel(
    nx, a, p, nu, li, m, s, ut, u, pc,
    cm, bct, a0c, br, fr, gp, bp, grs, rb1, rb2, rb3, rb4, rp, rrs, bq, bsw, bsum, bz, w, up, send, recv,
):
    n = nx * nx
    zc, part = n // 2, nx - 1
    r, c = lax.axis_index("row"), lax.axis_index("col")
    y, x = lax.div(r, nx), lax.rem(r, nx)
    z, k = lax.div(c, 2), lax.rem(c, 2)
    partner = c + 1 - 2 * k

    def copy(src, dst, name, axis, index):
        pltpu.make_async_remote_copy(
            src_ref=src, dst_ref=dst, send_sem=send.at[SEM[name]], recv_sem=recv.at[SEM[name]],
            device_id={axis: index}, device_id_type=MESH,
        ).start()

    def wait(ref, name, sems=recv):
        pltpu.make_async_copy(ref, ref, sems.at[SEM[name]]).wait()

    rows = [lax.rem(r + j, n) for j in range(1, n)]
    cols = [lax.rem(c + j, n) for j in range(1, n)]
    cores = [lax.rem(c + 2 * j, n) for j in range(1, zc)]
    def near(v, way):
        one = v + 1 - 2 * lax.rem(v, 2)
        two = lax.rem(v - 1 + 2 * lax.rem(v, 2) + nx, nx)
        return jnp.where(way == 0, one, two)

    def line(zz):
        return lax.div(2 * zz, nx), pl.ds(lax.rem(2 * zz, nx), 2)

    own_line = line(z)

    barrier = pltpu.get_barrier_semaphore()
    for i in rows:
        pl.semaphore_signal(barrier, inc=1, device_id={"row": i}, device_id_type=MESH)
    for i in cols:
        pl.semaphore_signal(barrier, inc=1, device_id={"col": i}, device_id_type=MESH)
    pl.semaphore_wait(barrier, 2 * n - 2)

    every = slice(None)
    steps = 4 if nx == 4 else 2

    def plan(first, way):
        ya, xa = near(y, way), near(x, way)
        yb, xb = near(y, 1 - way), near(x, 1 - way)
        along_x, along_y = [([(y, x)], y * nx + xa)], [([(y, x)], ya * nx + x)]
        if nx == 4:
            along_x.append(([(y, x), (y, xa)], y * nx + xb))
            along_y.append(([(y, x), (ya, x)], yb * nx + x))
        if first == 0:
            along_x.append(([(y, every)], ya * nx + x))
            if nx == 4:
                along_x.append(([(y, every), (ya, every)], yb * nx + x))
            return along_x
        along_y.append(([(every, x)], y * nx + xa))
        if nx == 4:
            along_y.append(([(every, x), (every, xa)], y * nx + xb))
        return along_y

    full_parts = [((kk, h), plan(h, kk)) for kk in range(2) for h in range(2)]
    half_parts = [(h, plan(h, k)) for h in range(2)]

    def full_got(ref, step):
        return (ref.at[:, 0, 0], ref.at[:, 0, pl.ds(0, 2)], ref.at[:, 0], ref.at[:, pl.ds(0, 2)])[
            step if nx == 4 else 2 * step
        ]

    def half_got(it, step):
        ref = cm.at[it, k]
        return (ref.at[0, 0], ref.at[0, pl.ds(0, 2)], ref.at[0], ref.at[pl.ds(0, 2)])[
            step if nx == 4 else 2 * step
        ]

    def full(ref, item, step):
        if step > steps:
            return
        if step > 0:
            wait(full_got(ref, step - 1), (item, step - 1))
        if step == steps:
            return
        for (kk, h), moves in full_parts:
            pieces, target = moves[step]
            for v, u_ in pieces:
                copy(ref.at[kk, v, u_, h], ref.at[kk, v, u_, h], (item, step), "row", target)

    def half(it, step):
        if step > steps:
            return
        if step > 0:
            wait(half_got(it, step - 1), (it, step - 1))
        if step == steps:
            copy(cm.at[it, k], cm.at[it, k], (it, 4), "col", partner)
            return
        for h, moves in half_parts:
            pieces, target = moves[step]
            for v, u_ in pieces:
                copy(cm.at[it, k, v, u_, h], cm.at[it, k, v, u_, h], (it, step), "row", target)

    def half_end(it):
        wait(cm.at[it, 1 - k], (it, 4))

    halves = (rb1, rb2, rb3, rb4)

    def reduce_step(step):
        if nx == 2 and step in (0, 2):
            return
        for kk in range(2):
            for h in range(2):
                at = 2 * kk + h
                on_y = (h == 0) == (step < 2)
                v = y if on_y else x
                near_a, near_b = near(v, kk), near(v, 1 - kk)
                goal = near_b if step % 2 == 0 else near_a
                target = goal * nx + x if on_y else y * nx + goal
                taken = [goal, near(goal, kk)] if step % 2 == 0 else [goal]
                for j, index in enumerate(taken):
                    other = every if step < 2 else (x if on_y else y)
                    src = bp.at[kk, index, other, h] if on_y else bp.at[kk, other, index, h]
                    dst = halves[step].at[at, j] if step % 2 == 0 else halves[step].at[at]
                    copy(src, dst, ("rs", step), "row", target)

    def reduce_add(step):
        if nx == 2 and step in (0, 2):
            return
        wait(halves[step], ("rs", step))
        for kk in range(2):
            for h in range(2):
                at = 2 * kk + h
                on_y = (h == 0) == (step < 2)
                v = y if on_y else x
                kept = [v, near(v, kk)] if step % 2 == 0 else [v]
                for j, index in enumerate(kept):
                    other = every if step < 2 else (x if on_y else y)
                    got = halves[step][at, j] if step % 2 == 0 else halves[step][at]
                    where_ = (kk, index, other, h) if on_y else (kk, other, index, h)
                    bp[where_] += got

    def whole(ref):
        return ref[...].reshape(512, 512)

    panel = whole(p)
    mine = pl.ds(pl.multiple_of(k * 256, 256), 256)
    w[...] = panel
    gp[...] = dotg(w[:, mine], panel, 0, 0).reshape(gp.shape)
    for i in rows:
        copy(gp.at[lax.div(i, nx), lax.rem(i, nx)], grs.at[r], "g_rs", "row", i)
    grs[r] = gp[y, x]

    @pl.when(r == c)
    def _():
        for i in rows:
            v, h = lax.div(i, nx), lax.rem(i, nx)
            copy(p.at[:, v, h], pc.at[:, v, h], "pc_s", "row", i)
        pc[:, y, x] = p[:, y, x]

    @pl.when(c == 0)
    def _():
        for j in cols:
            kk, (v, h) = lax.rem(j, 2), line(lax.div(j, 2))
            copy(a.at[kk, v, h], fr.at[kk, v, h], "fr_s", "col", j)
        fr[(k, *own_line)] = a[(k, *own_line)]

    bp[...] = dot3(panel, whole(a), 0, 0).reshape(bp.shape)
    reduce_step(0 if nx == 4 else 1)

    wait(grs.at[pl.ds(0, n - 1)], "g_rs")
    cm[G, k, y, x] = jnp.sum(grs[...], axis=0)
    where = [(h + 2 * q * max(1, zc // 4), h, q) for h in range(2) for q in range(2)]
    reducer = functools.reduce(jnp.logical_or, [c == dst for dst, *_ in where])

    def b_step(step):
        def run():
            if nx == 2 and step == 2:
                reduce_add(1)
                reduce_step(3)
            elif nx == 4:
                reduce_add(step - 1)
                reduce_step(step)
        return run

    def b_done():
        reduce_add(3)
        bct[:, y, x] = bp[:, y, x]
        full(bct, "bc", 0)

        @pl.when(c == 0)
        def _():
            for j in cols:
                kk = lax.rem(j, 2)
                copy(bct.at[kk, y, x], cm.at[B0, kk, y, x], "b0_s", "col", j)
            cm[B0, k, y, x] = bct[k, y, x]

    def pc_start():
        @pl.when(r != c)
        def _():
            wait(pc.at[:, y, x], "pc_s")

        full(pc, "pc", 0)

    def a0_start():
        @pl.when(r != 0)
        def _():
            wait(a0c.at[:, y, x], "a0_s")

        full(a0c, "a0", 0)

        @pl.when(c == 0)
        def _():
            for j in cols:
                kk = lax.rem(j, 2)
                copy(a0c.at[kk, y, x], cm.at[F0, kk, y, x], "f0_s", "col", j)
            cm[F0, k, y, x] = a0c[k, y, x]

    def p0_start():
        @pl.when(r != 0)
        def _():
            wait(cm.at[P0, k, y, x], "p0_s")

        half(P0, 0)

    def fr_start():
        @pl.when(c != 0)
        def _():
            wait(fr.at[(k, *own_line)], "fr_s")

        for j in cores:
            copy(fr.at[(k, *own_line)], fr.at[(k, *own_line)], "fr_g", "col", j)

    def fr_swap():
        wait(bz.at[pl.ds(0, zc - 1)], "fr_g")
        copy(fr.at[k], fr.at[k], "fr_w", "col", partner)

    def bq_start():
        full(pc, "pc", steps)
        bq[...] = dot3(whole(a), whole(pc), 1, 0).reshape(bq.shape)
        copy(bq.at[1 - k], bsw, "bq_w", "col", partner)

    def rp_start():
        rp[...] = dot3(bct[:, y, x].reshape(512 // n, 512), whole(pc), 1, 0).reshape(rp.shape)
        for dst, h, q in where:
            @pl.when(c != dst)
            def _():
                copy(rp.at[h, q], rrs.at[c], "r_rs", "col", dst)

            @pl.when(c == dst)
            def _():
                rrs[c] = rp[h, q]

    def br_reduce():
        wait(bsw, "bq_w")
        bsum[...] = bq[k] + bsw[...]
        for j in cores:
            copy(bsum.at[line(lax.div(j, 2))], bz.at[z], "bz", "col", j)
        bz[z] = bsum[own_line]

    def br_start():
        wait(bz.at[pl.ds(0, zc - 1)], "bz")
        br[(k, *own_line)] = jnp.sum(bz[...], axis=0)
        for j in cores:
            copy(br.at[(k, *own_line)], br.at[(k, *own_line)], "br_g", "col", j)

    def br_swap():
        wait(bz.at[pl.ds(0, zc - 1)], "br_g")
        copy(br.at[k], br.at[k], "br_w", "col", partner)

    def r_reduce():
        for dst, h, q in where:
            @pl.when(c == dst)
            def _():
                wait(rrs.at[pl.ds(0, n - 1)], "r_rs")
                cm[R, h, y, x, q] = jnp.sum(rrs[...], axis=0)
                for j in cores:
                    copy(cm.at[R, h, y, x, q], cm.at[R, h, y, x, q], "r_b", "col", j)

    def r_start():
        @pl.when(reducer)
        def _():
            wait(rrs.at[0], "r_b")

        @pl.when(jnp.logical_not(reducer))
        def _():
            wait(rrs.at[pl.ds(0, 2)], "r_b")

        half(R, 0)

    def b0_start():
        @pl.when(c != 0)
        def _():
            wait(cm.at[B0, k, y, x], "b0_s")

        half(B0, 0)

    def f0_start():
        @pl.when(c != 0)
        def _():
            wait(cm.at[F0, k, y, x], "f0_s")

        half(F0, 0)

    def f(ref, item, step):
        return lambda: full(ref, item, step) if step < steps else None

    def g(it, step):
        return lambda: half(it, step)

    def spread_p0():
        @pl.when(r == 0)
        def _():
            for i in rows:
                v, h = lax.div(i, nx), lax.rem(i, nx)
                copy(p.at[k, v, h], cm.at[P0, k, v, h], "p0_s", "row", i)
            cm[P0, k, y, x] = p[k, y, x]

    def spread_a0(part):
        def run():
            @pl.when(r == 0)
            def _():
                for i in rows[part::5]:
                    v, h = lax.div(i, nx), lax.rem(i, nx)
                    copy(a.at[:, v, h], a0c.at[:, v, h], "a0_s", "row", i)
                if part == 0:
                    a0c[:, y, x] = a[:, y, x]
        return run

    before = [
        g(G, 0), pc_start, spread_a0(0), g(G, 1), b_step(1), fr_start, spread_a0(1),
        g(G, 2), f(pc, "pc", 1), b_step(2), spread_a0(2), g(G, 3), f(pc, "pc", 2), b_step(3),
        spread_a0(3), g(G, 4), f(pc, "pc", 3), b_done, spread_a0(4), spread_p0,
    ]
    for action in before:
        action()

    hooks = [
        [],
        [bq_start],
        [rp_start, f(bct, "bc", 1), a0_start],
        [f(bct, "bc", 2), p0_start, b0_start],
        [r_reduce, br_reduce, f(a0c, "a0", 1)],
        [f(bct, "bc", 3), g(P0, 1), g(B0, 1)],
        [r_start, f(a0c, "a0", 2), f0_start],
        [g(P0, 2), g(B0, 2), g(R, 1)],
        [f(a0c, "a0", 3), g(F0, 1)],
        [g(P0, 3), g(R, 2), g(B0, 3)],
        [g(F0, 2)],
        [g(P0, 4), g(R, 3), g(B0, 4), br_start],
        [g(F0, 3), fr_swap],
        [g(R, 4)],
        [g(F0, 4)],
        [],
    ]

    left = list(hooks)

    def pause():
        for action in left.pop(0):
            action()

    half_end(G)
    w[...] = cm[G].reshape(512, 512)
    up[...] = jnp.zeros((512, 512), F32)
    li[...] = jnp.zeros((512, 512), F32)
    for b in range(4):
        factor_block(b, w, up, li, pause)
        pause()
    nu[...] = -up[...]

    eye = (
        lax.broadcasted_iota(jnp.int32, (512, 512), 0)
        == lax.broadcasted_iota(jnp.int32, (512, 512), 1)
    ).astype(F32)
    lis = split(li[...])
    half_end(P0)
    m[...] = eye + dot3(lis, cm[P0].reshape(512, 512), 1, 1)
    full(a0c, "a0", steps)
    full(bct, "bc", steps)
    ut[...] = dot3(lis, whole(bct), 1, 0) + whole(a0c)
    br_swap()
    half_end(B0)
    half_end(F0)
    s[...] = dot3(lis, cm[B0].reshape(512, 512), 1, 0)
    s[...] += s[...].T + cm[F0].reshape(512, 512)
    half_end(R)
    s[...] += dot3(lis, dot3(cm[R].reshape(512, 512), lis, 1, 1), 1, 0)
    wait(br.at[1 - k], "br_w")
    wait(fr.at[1 - k], "fr_w")
    u[...] = dot3(whole(br), lis, 1, 1) + whole(fr)

    scattered = grs.at[pl.ds(0, n - 1)]

    slices = cm.at[:, :, 0, pl.ds(0, 3)] if nx == 4 else cm.at[pl.ds(0, 3), :, 0, 0]

    def wait_slices(name, sems):
        wait(slices, name, sems)

    @pl.when(r == c)
    def _():
        wait_slices( "pc_s", send)

    @pl.when(r == 0)
    def _():
        wait(scattered, "p0_s", send)
        wait_slices( "a0_s", send)

    @pl.when(c == 0)
    def _():
        wait_slices( "fr_s", send)
        wait(scattered, "b0_s", send)
        wait(scattered, "f0_s", send)

    wait(scattered, "g_rs", send)
    for step in range(steps):
        for item in ("pc", "bc", "a0"):
            wait(full_got(pc, step), (item, step), send)
        for it in range(5):
            wait(half_got(it, step), (it, step), send)
    for step in range(4):
        if nx == 4 or step in (1, 3):
            wait(halves[step], ("rs", step), send)
    for name in ("bq_w", "br_w", "fr_w", *((it, 4) for it in range(5))):
        wait(cm.at[0, 0], name, send)
    for name in ("bz", "br_g", "fr_g"):
        wait(bz.at[pl.ds(0, zc - 1)], name, send)

    @pl.when(reducer)
    def _():
        wait(rrs.at[pl.ds(0, 3)], "r_rs", send)
        wait(rrs.at[pl.ds(0, zc - 1)], "r_b", send)

    @pl.when(jnp.logical_not(reducer))
    def _():
        wait(rrs.at[pl.ds(0, 4)], "r_rs", send)


def final_kernel(a, p, li, m, s, ut, u, pc, out, xx, e):
    r, c = lax.axis_index("row"), lax.axis_index("col")
    eye = (
        lax.broadcasted_iota(jnp.int32, (512, 512), 0)
        == lax.broadcasted_iota(jnp.int32, (512, 512), 1)
    ).astype(F32)
    start = 0.9
    e[...] = eye - start * m[...]
    xx[...] = start * (eye + e[...])

    def more(state):
        step, now = state
        return jnp.logical_and(step < 48, now > 1e-3)

    def square(state):
        step, _ = state
        es = split(e[...])
        ee = dot3(es, es, 1, 0)
        e[...] = ee
        xx[...] += dot3(xx[...], ee, 1, 0)
        return step + 1, jnp.sum(ee * ee)

    lax.while_loop(more, square, (jnp.int32(0), jnp.float32(1.0)))
    xs = split(xx[...])
    rest = eye - dot3(m[...], xs, 1, 0)
    inv = xx[...] + dot3(xs, rest, 1, 0)
    nis = split(dot3(inv, li[...], 1, 0))
    yts = split(jnp.where(c == 0, eye, dot3(nis, pc[...], 1, 1)))
    zt = ut[...] - dot3(s[...], yts, 1, 0)
    y = jnp.where(r == 0, eye, dot3(p[...], nis, 1, 1))
    out[...] = a[...] - dot3(y, zt, 1, 0) - dot3(u[...], yts, 1, 0)


def solution(mesh):
    n = mesh.shape["row"]
    nx = {4: 2, 16: 4}[n]
    zc, rr = n // 2, 128 // n
    vm = pl.BlockSpec(memory_space=pltpu.VMEM)
    sq = jax.ShapeDtypeStruct((512, 512), F32)
    shape = (2, nx, nx, 2, rr, 512)

    def scratch(*lead):
        return pltpu.VMEM((*lead, 512), F32)

    def step(trailing, panel):
        nu, li, m, s, ut, u, pc = pl.pallas_call(
            functools.partial(main_kernel, nx),
            out_shape=[sq] * 6 + [jax.ShapeDtypeStruct(shape, F32)],
            in_specs=[vm] * 2,
            out_specs=[vm] * 7,
            scratch_shapes=[
                scratch(5, *shape[:-1]),
                scratch(*shape[:-1]),
                scratch(*shape[:-1]),
                scratch(*shape[:-1]),
                scratch(*shape[:-1]),
                scratch(*shape[1:-1]),
                scratch(*shape[:-1]),
                scratch(n, 2, rr),
                scratch(4, 2, nx, rr),
                scratch(4, nx, rr),
                scratch(4, 2, rr),
                scratch(4, rr),
                scratch(2, 2, rr),
                scratch(n, rr),
                scratch(*shape[:-1]),
                scratch(*shape[1:-1]),
                scratch(*shape[1:-1]),
                scratch(zc, 2, 2, rr),
                scratch(512),
                scratch(512),
                pltpu.SemaphoreType.DMA((len(NAMES),)),
                pltpu.SemaphoreType.DMA((len(NAMES),)),
            ],
            compiler_params=pltpu.CompilerParams(collective_id=0, has_side_effects=True, vmem_limit_bytes=34 << 20),
            name="exchange_factor",
        )(trailing.reshape(shape), panel.reshape(shape))
        out = pl.pallas_call(
            final_kernel,
            out_shape=sq,
            in_specs=[vm] * 8,
            out_specs=vm,
            scratch_shapes=[pltpu.VMEM((512, 512), F32)] * 2,
            compiler_params=pltpu.CompilerParams(vmem_limit_bytes=30 << 20),
            name="update",
        )(trailing, panel, li, m, s, ut, u, pc.reshape(512, 512))
        return out, nu

    return jax.shard_map(
        step, mesh=mesh, in_specs=(P("row", "col"), P("row", None)),
        out_specs=(P("row", "col"), P()), check_vma=False,
    )
```

```python
import functools
import jax
import jax.numpy as jnp
from jax import lax
from jax.experimental import pallas as pl
from jax.experimental.pallas import tpu as pltpu
from jax.sharding import PartitionSpec as P

HI = lax.Precision.HIGHEST
F32 = jnp.float32
BF16 = jnp.bfloat16
MESH = pl.DeviceIdType.MESH
G, P0, B0, F0, R = range(5)


def dotg(a, b, ca, cb):
    return lax.dot_general(
        a, b, (((ca,), (cb,)), ((), ())), precision=HI, preferred_element_type=F32
    )


def split(x):
    high = x.astype(BF16)
    return high, (x - high.astype(F32)).astype(BF16)


def dot3(a, b, ca, cb):
    ah, al = a if isinstance(a, tuple) else split(a)
    bh, bl = b if isinstance(b, tuple) else split(b)
    dims = (((ca,), (cb,)), ((), ()))
    d = functools.partial(lax.dot_general, dimension_numbers=dims, preferred_element_type=F32)
    return d(ah, bh) + (d(ah, bl) + d(al, bh))


def bc(x):
    return jnp.broadcast_to(x, (8, 128))


def leaf(d, pause):
    sub = lax.broadcasted_iota(jnp.int32, (8, 128), 0)
    lane = lax.broadcasted_iota(jnp.int32, (8, 128), 1)
    d = list(d)
    inv = [(lane == sub + 8 * q).astype(F32) for q in range(16)]
    upper, lower_inv = [], []
    for q in range(16):
        cb = [bc(d[q][:, 8 * q + j : 8 * q + j + 1]) for j in range(8)]
        mul = [[bc(d[p][:, 8 * q + j : 8 * q + j + 1]) for j in range(8)] for p in range(q + 1, 16)]
        zd, zi = d[q], inv[q]
        ud = jnp.zeros((8, 128), F32)
        ui = ud
        for j in range(8):
            pivot = bc(cb[j][j : j + 1, :])
            r = 1.0 / pivot
            rs = lax.rsqrt(pivot)
            rd, ri = bc(zd[j : j + 1, :]), bc(zi[j : j + 1, :])
            mine = sub == j
            ud, ui = jnp.where(mine, rd * rs, ud), jnp.where(mine, ri * rs, ui)
            pd, pi = rd * r, ri * r
            zd = jnp.where(mine, pd, zd - cb[j] * pd)
            zi = jnp.where(mine, pi, zi - cb[j] * pi)
            for k in range(j + 1, 8):
                t = bc(cb[k][j : j + 1, :]) * r
                cb[k] = jnp.where(mine, t, cb[k] - cb[j] * t)
        upper.append(jnp.where(lane >= sub + 8 * q, ud, 0.0))
        lower_inv.append(ui)
        zds = [bc(zd[j : j + 1, :]) for j in range(8)]
        zis = [bc(zi[j : j + 1, :]) for j in range(8)]
        for p in range(q + 1, 16):
            m = mul[p - q - 1]
            x, y = d[p], inv[p]
            for j in range(8):
                x, y = x - m[j] * zds[j], y - m[j] * zis[j]
            d[p], inv[p] = x, y
        if q in (3, 7, 11):
            pause()
    return upper, lower_inv


def factor_block(b, w, u, li, pause):
    s, e = 128 * b, 128 * b + 128
    upper, lower_inv = leaf([w[s + 8 * q : s + 8 * q + 8, s:e] for q in range(16)], pause)
    for q in range(16):
        u[s + 8 * q : s + 8 * q + 8, s:e] = upper[q]
        li[s + 8 * q : s + 8 * q + 8, s:e] = lower_inv[q]
    lb = li[s:e, s:e]
    if b < 3:
        u[s:e, e:] = dotg(lb, w[s:e, e:], 1, 0)
    if b > 0:
        li[s:e, :s] = dotg(lb, li[s:e, :s], 1, 0)
    if b < 3:
        ut = u[s:e, e:]
        w[e:, e:] -= dotg(ut, ut, 0, 0)
        li[e:, :e] -= dotg(ut, li[s:e, :e], 0, 0)


NAMES = ["pc_s", "p0_s", "a0_s", "fr_s", "g_rs", "b0_s", "f0_s", "r_rs"]
NAMES += ["r_b", "bq_w", "bz", "br_g", "br_w", "fr_g", "fr_w"]
NAMES += [(item, step) for item in ("pc", "bc", "a0", "rs") for step in range(4)]
NAMES += [(item, step) for item in range(5) for step in range(5)]
SEM = {name: i for i, name in enumerate(NAMES)}


def main_kernel(
    nx, a_in, p_in, nu, li, m, s, ut, u, pc,
    a, p, load, cm, bct, a0c, br, fr, gp, bp, grs, rb1, rb2, rb3, rb4, rp, rrs, bq, bsw, bsum, bz, w, up, send, recv,
):
    n = nx * nx
    zc, part = n // 2, nx - 1
    r, c = lax.axis_index("row"), lax.axis_index("col")
    y, x = lax.div(r, nx), lax.rem(r, nx)
    z, k = lax.div(c, 2), lax.rem(c, 2)
    partner = c + 1 - 2 * k

    def copy(src, dst, name, axis, index):
        pltpu.make_async_remote_copy(
            src_ref=src, dst_ref=dst, send_sem=send.at[SEM[name]], recv_sem=recv.at[SEM[name]],
            device_id={axis: index}, device_id_type=MESH,
        ).start()

    def wait(ref, name, sems=recv):
        pltpu.make_async_copy(ref, ref, sems.at[SEM[name]]).wait()

    rows = [lax.rem(r + j, n) for j in range(1, n)]
    cols = [lax.rem(c + j, n) for j in range(1, n)]
    cores = [lax.rem(c + 2 * j, n) for j in range(1, zc)]
    def near(v, way):
        one = v + 1 - 2 * lax.rem(v, 2)
        two = lax.rem(v - 1 + 2 * lax.rem(v, 2) + nx, nx)
        return jnp.where(way == 0, one, two)

    def line(zz):
        return lax.div(2 * zz, nx), pl.ds(lax.rem(2 * zz, nx), 2)

    own_line = line(z)

    loads = [pltpu.make_async_copy(p_in, p, load.at[0]), pltpu.make_async_copy(a_in, a, load.at[1])]
    for piece in loads:
        piece.start()
    barrier = pltpu.get_barrier_semaphore()
    for i in rows:
        pl.semaphore_signal(barrier, inc=1, device_id={"row": i}, device_id_type=MESH)
    for i in cols:
        pl.semaphore_signal(barrier, inc=1, device_id={"col": i}, device_id_type=MESH)

    every = slice(None)
    steps = 4 if nx == 4 else 2

    def plan(first, way):
        ya, xa = near(y, way), near(x, way)
        yb, xb = near(y, 1 - way), near(x, 1 - way)
        along_x, along_y = [([(y, x)], y * nx + xa)], [([(y, x)], ya * nx + x)]
        if nx == 4:
            along_x.append(([(y, x), (y, xa)], y * nx + xb))
            along_y.append(([(y, x), (ya, x)], yb * nx + x))
        if first == 0:
            along_x.append(([(y, every)], ya * nx + x))
            if nx == 4:
                along_x.append(([(y, every), (ya, every)], yb * nx + x))
            return along_x
        along_y.append(([(every, x)], y * nx + xa))
        if nx == 4:
            along_y.append(([(every, x), (every, xa)], y * nx + xb))
        return along_y

    full_parts = [((kk, h), plan(h, kk)) for kk in range(2) for h in range(2)]
    half_parts = [(h, plan(h, k)) for h in range(2)]

    def full_got(ref, step):
        return (ref.at[:, 0, 0], ref.at[:, 0, pl.ds(0, 2)], ref.at[:, 0], ref.at[:, pl.ds(0, 2)])[
            step if nx == 4 else 2 * step
        ]

    def half_got(it, step):
        ref = cm.at[it, k]
        return (ref.at[0, 0], ref.at[0, pl.ds(0, 2)], ref.at[0], ref.at[pl.ds(0, 2)])[
            step if nx == 4 else 2 * step
        ]

    def full(ref, item, step):
        if step > steps:
            return
        if step > 0:
            wait(full_got(ref, step - 1), (item, step - 1))
        if step == steps:
            return
        for (kk, h), moves in full_parts:
            pieces, target = moves[step]
            for v, u_ in pieces:
                copy(ref.at[kk, v, u_, h], ref.at[kk, v, u_, h], (item, step), "row", target)

    def half(it, step):
        if step > steps:
            return
        if step > 0:
            wait(half_got(it, step - 1), (it, step - 1))
        if step == steps:
            copy(cm.at[it, k], cm.at[it, k], (it, 4), "col", partner)
            return
        for h, moves in half_parts:
            pieces, target = moves[step]
            for v, u_ in pieces:
                copy(cm.at[it, k, v, u_, h], cm.at[it, k, v, u_, h], (it, step), "row", target)

    def half_end(it):
        wait(cm.at[it, 1 - k], (it, 4))

    halves = (rb1, rb2, rb3, rb4)

    def reduce_step(step):
        if nx == 2 and step in (0, 2):
            return
        for kk in range(2):
            for h in range(2):
                at = 2 * kk + h
                on_y = (h == 0) == (step < 2)
                v = y if on_y else x
                near_a, near_b = near(v, kk), near(v, 1 - kk)
                goal = near_b if step % 2 == 0 else near_a
                target = goal * nx + x if on_y else y * nx + goal
                taken = [goal, near(goal, kk)] if step % 2 == 0 else [goal]
                for j, index in enumerate(taken):
                    other = every if step < 2 else (x if on_y else y)
                    src = bp.at[kk, index, other, h] if on_y else bp.at[kk, other, index, h]
                    dst = halves[step].at[at, j] if step % 2 == 0 else halves[step].at[at]
                    copy(src, dst, ("rs", step), "row", target)

    def reduce_add(step):
        if nx == 2 and step in (0, 2):
            return
        wait(halves[step], ("rs", step))
        for kk in range(2):
            for h in range(2):
                at = 2 * kk + h
                on_y = (h == 0) == (step < 2)
                v = y if on_y else x
                kept = [v, near(v, kk)] if step % 2 == 0 else [v]
                for j, index in enumerate(kept):
                    other = every if step < 2 else (x if on_y else y)
                    got = halves[step][at, j] if step % 2 == 0 else halves[step][at]
                    where_ = (kk, index, other, h) if on_y else (kk, other, index, h)
                    bp[where_] += got

    def whole(ref):
        return ref[...].reshape(512, 512)

    loads[0].wait()
    panel = whole(p)
    mine = pl.ds(pl.multiple_of(k * 256, 256), 256)
    w[...] = panel
    gp[...] = dotg(w[:, mine], panel, 0, 0).reshape(gp.shape)
    loads[1].wait()
    bp[...] = dot3(panel, whole(a), 0, 0).reshape(bp.shape)
    pl.semaphore_wait(barrier, 2 * n - 2)
    for i in rows:
        copy(gp.at[lax.div(i, nx), lax.rem(i, nx)], grs.at[r], "g_rs", "row", i)
    grs[r] = gp[y, x]

    @pl.when(r == c)
    def _():
        for i in rows:
            v, h = lax.div(i, nx), lax.rem(i, nx)
            copy(p.at[:, v, h], pc.at[:, v, h], "pc_s", "row", i)
        pc[:, y, x] = p[:, y, x]

    @pl.when(c == 0)
    def _():
        for j in cols:
            kk, (v, h) = lax.rem(j, 2), line(lax.div(j, 2))
            copy(a.at[kk, v, h], fr.at[kk, v, h], "fr_s", "col", j)
        fr[(k, *own_line)] = a[(k, *own_line)]

    reduce_step(0 if nx == 4 else 1)

    wait(grs.at[pl.ds(0, n - 1)], "g_rs")
    cm[G, k, y, x] = jnp.sum(grs[...], axis=0)
    where = [(h + 2 * q * max(1, zc // 4), h, q) for h in range(2) for q in range(2)]
    reducer = functools.reduce(jnp.logical_or, [c == dst for dst, *_ in where])

    def b_step(step):
        def run():
            if nx == 2 and step == 2:
                reduce_add(1)
                reduce_step(3)
            elif nx == 4:
                reduce_add(step - 1)
                reduce_step(step)
        return run

    def b_done():
        reduce_add(3)
        bct[:, y, x] = bp[:, y, x]
        full(bct, "bc", 0)

        @pl.when(c == 0)
        def _():
            for j in cols:
                kk = lax.rem(j, 2)
                copy(bct.at[kk, y, x], cm.at[B0, kk, y, x], "b0_s", "col", j)
            cm[B0, k, y, x] = bct[k, y, x]

    def pc_start():
        @pl.when(r != c)
        def _():
            wait(pc.at[:, y, x], "pc_s")

        full(pc, "pc", 0)

    def a0_start():
        @pl.when(r != 0)
        def _():
            wait(a0c.at[:, y, x], "a0_s")

        full(a0c, "a0", 0)

        @pl.when(c == 0)
        def _():
            for j in cols:
                kk = lax.rem(j, 2)
                copy(a0c.at[kk, y, x], cm.at[F0, kk, y, x], "f0_s", "col", j)
            cm[F0, k, y, x] = a0c[k, y, x]

    def p0_start():
        @pl.when(r != 0)
        def _():
            wait(cm.at[P0, k, y, x], "p0_s")

        half(P0, 0)

    def fr_start():
        @pl.when(c != 0)
        def _():
            wait(fr.at[(k, *own_line)], "fr_s")

        for j in cores:
            copy(fr.at[(k, *own_line)], fr.at[(k, *own_line)], "fr_g", "col", j)

    def fr_swap():
        wait(bz.at[pl.ds(0, zc - 1)], "fr_g")
        copy(fr.at[k], fr.at[k], "fr_w", "col", partner)

    def bq_start():
        full(pc, "pc", steps)
        bq[...] = dot3(whole(a), whole(pc), 1, 0).reshape(bq.shape)
        copy(bq.at[1 - k], bsw, "bq_w", "col", partner)

    def rp_start():
        rp[...] = dot3(bct[:, y, x].reshape(512 // n, 512), whole(pc), 1, 0).reshape(rp.shape)
        for dst, h, q in where:
            @pl.when(c != dst)
            def _():
                copy(rp.at[h, q], rrs.at[c], "r_rs", "col", dst)

            @pl.when(c == dst)
            def _():
                rrs[c] = rp[h, q]

    def br_reduce():
        wait(bsw, "bq_w")
        bsum[...] = bq[k] + bsw[...]
        for j in cores:
            copy(bsum.at[line(lax.div(j, 2))], bz.at[z], "bz", "col", j)
        bz[z] = bsum[own_line]

    def br_start():
        wait(bz.at[pl.ds(0, zc - 1)], "bz")
        br[(k, *own_line)] = jnp.sum(bz[...], axis=0)
        for j in cores:
            copy(br.at[(k, *own_line)], br.at[(k, *own_line)], "br_g", "col", j)

    def br_swap():
        wait(bz.at[pl.ds(0, zc - 1)], "br_g")
        copy(br.at[k], br.at[k], "br_w", "col", partner)

    def r_reduce():
        for dst, h, q in where:
            @pl.when(c == dst)
            def _():
                wait(rrs.at[pl.ds(0, n - 1)], "r_rs")
                cm[R, h, y, x, q] = jnp.sum(rrs[...], axis=0)
                for j in cores:
                    copy(cm.at[R, h, y, x, q], cm.at[R, h, y, x, q], "r_b", "col", j)

    def r_start():
        @pl.when(reducer)
        def _():
            wait(rrs.at[0], "r_b")

        @pl.when(jnp.logical_not(reducer))
        def _():
            wait(rrs.at[pl.ds(0, 2)], "r_b")

        half(R, 0)

    def b0_start():
        @pl.when(c != 0)
        def _():
            wait(cm.at[B0, k, y, x], "b0_s")

        half(B0, 0)

    def f0_start():
        @pl.when(c != 0)
        def _():
            wait(cm.at[F0, k, y, x], "f0_s")

        half(F0, 0)

    def f(ref, item, step):
        return lambda: full(ref, item, step) if step < steps else None

    def g(it, step):
        return lambda: half(it, step)

    def spread_p0():
        @pl.when(r == 0)
        def _():
            for i in rows:
                v, h = lax.div(i, nx), lax.rem(i, nx)
                copy(p.at[k, v, h], cm.at[P0, k, v, h], "p0_s", "row", i)
            cm[P0, k, y, x] = p[k, y, x]

    def spread_a0(part):
        def run():
            @pl.when(r == 0)
            def _():
                for i in rows[part::5]:
                    v, h = lax.div(i, nx), lax.rem(i, nx)
                    copy(a.at[:, v, h], a0c.at[:, v, h], "a0_s", "row", i)
                if part == 0:
                    a0c[:, y, x] = a[:, y, x]
        return run

    before = [
        g(G, 0), pc_start, spread_a0(0), g(G, 1), b_step(1), fr_start, spread_a0(1),
        g(G, 2), f(pc, "pc", 1), b_step(2), spread_a0(2), g(G, 3), f(pc, "pc", 2), b_step(3),
        spread_a0(3), g(G, 4), f(pc, "pc", 3), b_done, spread_a0(4), spread_p0,
    ]
    for action in before:
        action()

    hooks = [
        [],
        [bq_start],
        [rp_start, f(bct, "bc", 1), a0_start],
        [br_reduce, f(bct, "bc", 2), p0_start, b0_start],
        [r_reduce, f(a0c, "a0", 1)],
        [f(bct, "bc", 3), g(P0, 1), g(B0, 1)],
        [f(a0c, "a0", 2), f0_start],
        [g(P0, 2), g(B0, 2)],
        [r_start, f(a0c, "a0", 3), g(F0, 1)],
        [g(P0, 3), g(B0, 3), br_start],
        [g(F0, 2), g(R, 1)],
        [g(P0, 4), g(B0, 4), g(R, 2)],
        [g(F0, 3), fr_swap],
        [g(R, 3)],
        [g(F0, 4)],
        [g(R, 4)],
    ]

    left = list(hooks)

    def pause():
        for action in left.pop(0):
            action()

    half_end(G)
    w[...] = cm[G].reshape(512, 512)
    up[...] = jnp.zeros((512, 512), F32)
    li[...] = jnp.zeros((512, 512), F32)
    for b in range(4):
        factor_block(b, w, up, li, pause)
        pause()
    nu[...] = -up[...]

    eye = (
        lax.broadcasted_iota(jnp.int32, (512, 512), 0)
        == lax.broadcasted_iota(jnp.int32, (512, 512), 1)
    ).astype(F32)
    lis = split(li[...])
    half_end(P0)
    m[...] = eye + dot3(lis, cm[P0].reshape(512, 512), 1, 1)
    full(a0c, "a0", steps)
    full(bct, "bc", steps)
    ut[...] = dot3(lis, whole(bct), 1, 0) + whole(a0c)
    br_swap()
    half_end(B0)
    half_end(F0)
    s[...] = dot3(lis, cm[B0].reshape(512, 512), 1, 0)
    s[...] += s[...].T + cm[F0].reshape(512, 512)
    half_end(R)
    s[...] += dot3(lis, dot3(cm[R].reshape(512, 512), lis, 1, 1), 1, 0)
    wait(br.at[1 - k], "br_w")
    wait(fr.at[1 - k], "fr_w")
    u[...] = dot3(whole(br), lis, 1, 1) + whole(fr)

    scattered = grs.at[pl.ds(0, n - 1)]

    slices = cm.at[:, :, 0, pl.ds(0, 3)] if nx == 4 else cm.at[pl.ds(0, 3), :, 0, 0]

    def wait_slices(name, sems):
        wait(slices, name, sems)

    @pl.when(r == c)
    def _():
        wait_slices( "pc_s", send)

    @pl.when(r == 0)
    def _():
        wait(scattered, "p0_s", send)
        wait_slices( "a0_s", send)

    @pl.when(c == 0)
    def _():
        wait_slices( "fr_s", send)
        wait(scattered, "b0_s", send)
        wait(scattered, "f0_s", send)

    wait(scattered, "g_rs", send)
    for step in range(steps):
        for item in ("pc", "bc", "a0"):
            wait(full_got(pc, step), (item, step), send)
        for it in range(5):
            wait(half_got(it, step), (it, step), send)
    for step in range(4):
        if nx == 4 or step in (1, 3):
            wait(halves[step], ("rs", step), send)
    for name in ("bq_w", "br_w", "fr_w", *((it, 4) for it in range(5))):
        wait(cm.at[0, 0], name, send)
    for name in ("bz", "br_g", "fr_g"):
        wait(bz.at[pl.ds(0, zc - 1)], name, send)

    @pl.when(reducer)
    def _():
        wait(rrs.at[pl.ds(0, 3)], "r_rs", send)
        wait(rrs.at[pl.ds(0, zc - 1)], "r_b", send)

    @pl.when(jnp.logical_not(reducer))
    def _():
        wait(rrs.at[pl.ds(0, 4)], "r_rs", send)


def final_kernel(a, p, nu, li, m, s, ut, u, pc, out, band, xx, e, save):
    top = pltpu.make_async_copy(nu, band, save.at[4])
    top.start()
    r, c = lax.axis_index("row"), lax.axis_index("col")
    eye = (
        lax.broadcasted_iota(jnp.int32, (512, 512), 0)
        == lax.broadcasted_iota(jnp.int32, (512, 512), 1)
    ).astype(F32)
    start = 0.9
    e[...] = eye - start * m[...]
    xx[...] = start * (eye + e[...])

    def more(state):
        step, now = state
        return jnp.logical_and(step < 48, now > 1e-3)

    def square(state):
        step, _ = state
        es = split(e[...])
        ee = dot3(es, es, 1, 0)
        e[...] = ee
        xx[...] += dot3(xx[...], ee, 1, 0)
        return step + 1, jnp.sum(ee * ee)

    lax.while_loop(more, square, (jnp.int32(0), jnp.float32(1.0)))
    xs = split(xx[...])
    rest = eye - dot3(m[...], xs, 1, 0)
    inv = xx[...] + dot3(xs, rest, 1, 0)
    nis = split(dot3(inv, li[...], 1, 0))
    yts = split(jnp.where(c == 0, eye, dot3(nis, pc[...], 1, 1)))
    zts = split(ut[...] - dot3(s[...], yts, 1, 0))
    xx[...] = jnp.where(r == 0, eye, dot3(p[...], nis, 1, 1))
    saves = []
    for q in range(4):
        part = pl.ds(128 * q, 128)
        e[part] = a[part] - dot3(xx[part], zts, 1, 0) - dot3(u[part], yts, 1, 0)
        saves.append(pltpu.make_async_copy(e.at[part], out.at[part], save.at[q]))
        saves[-1].start()
    for copy in [top, *saves]:
        copy.wait()


def solution(mesh):
    n = mesh.shape["row"]
    nx = {4: 2, 16: 4}[n]
    zc, rr = n // 2, 128 // n
    vm = pl.BlockSpec(memory_space=pltpu.VMEM)
    hbm = pl.BlockSpec(memory_space=pltpu.HBM)
    sq = jax.ShapeDtypeStruct((512, 512), F32)
    shape = (2, nx, nx, 2, rr, 512)

    def scratch(*lead):
        return pltpu.VMEM((*lead, 512), F32)

    def step(trailing, panel):
        nu, li, m, s, ut, u, pc = pl.pallas_call(
            functools.partial(main_kernel, nx),
            out_shape=[sq] * 6 + [jax.ShapeDtypeStruct(shape, F32)],
            in_specs=[hbm] * 2,
            out_specs=[vm] * 7,
            scratch_shapes=[
                scratch(*shape[:-1]),
                scratch(*shape[:-1]),
                pltpu.SemaphoreType.DMA((2,)),
                scratch(5, *shape[:-1]),
                scratch(*shape[:-1]),
                scratch(*shape[:-1]),
                scratch(*shape[:-1]),
                scratch(*shape[:-1]),
                scratch(*shape[1:-1]),
                scratch(*shape[:-1]),
                scratch(n, 2, rr),
                scratch(4, 2, nx, rr),
                scratch(4, nx, rr),
                scratch(4, 2, rr),
                scratch(4, rr),
                scratch(2, 2, rr),
                scratch(n, rr),
                scratch(*shape[:-1]),
                scratch(*shape[1:-1]),
                scratch(*shape[1:-1]),
                scratch(zc, 2, 2, rr),
                scratch(512),
                scratch(512),
                pltpu.SemaphoreType.DMA((len(NAMES),)),
                pltpu.SemaphoreType.DMA((len(NAMES),)),
            ],
            compiler_params=pltpu.CompilerParams(collective_id=0, has_side_effects=True, vmem_limit_bytes=34 << 20),
            name="exchange_factor",
        )(
            pltpu.with_memory_space_constraint(trailing.reshape(shape), pltpu.HBM),
            pltpu.with_memory_space_constraint(panel.reshape(shape), pltpu.HBM),
        )
        return pl.pallas_call(
            final_kernel,
            out_shape=[sq, sq],
            in_specs=[vm] * 9,
            out_specs=[hbm] * 2,
            scratch_shapes=[pltpu.VMEM((512, 512), F32)] * 2 + [pltpu.SemaphoreType.DMA((5,))],
            compiler_params=pltpu.CompilerParams(vmem_limit_bytes=30 << 20),
            name="update",
        )(trailing, panel, nu, li, m, s, ut, u, pc.reshape(512, 512))

    return jax.shard_map(
        step, mesh=mesh, in_specs=(P("row", "col"), P("row", None)),
        out_specs=(P("row", "col"), P()), check_vma=False,
    )
```

```python
import functools
import jax
import jax.numpy as jnp
from jax import lax
from jax.experimental import pallas as pl
from jax.experimental.pallas import tpu as pltpu
from jax.sharding import PartitionSpec as P

HI = lax.Precision.HIGHEST
F32 = jnp.float32
BF16 = jnp.bfloat16
MESH = pl.DeviceIdType.MESH
G, P0, B0, F0, R = range(5)


def dotg(a, b, ca, cb):
    return lax.dot_general(
        a, b, (((ca,), (cb,)), ((), ())), precision=HI, preferred_element_type=F32
    )


def split(x):
    high = x.astype(BF16)
    return high, (x - high.astype(F32)).astype(BF16)


def dot3(a, b, ca, cb):
    ah, al = a if isinstance(a, tuple) else split(a)
    bh, bl = b if isinstance(b, tuple) else split(b)
    dims = (((ca,), (cb,)), ((), ()))
    d = functools.partial(lax.dot_general, dimension_numbers=dims, preferred_element_type=F32)
    return d(ah, bh) + (d(ah, bl) + d(al, bh))


def lower_times(lower, x, cb):
    xs = split(x)
    head = tuple(v[:256] if cb == 0 else v[:, :256] for v in xs)
    return jnp.concatenate([dot3(lower[0], head, 1, cb), dot3(lower[1], xs, 1, cb)], axis=0)


def times_upper(x, lower):
    xs = split(x)
    head = tuple(v[:, :256] for v in xs)
    return jnp.concatenate([dot3(head, lower[0], 1, 1), dot3(xs, lower[1], 1, 1)], axis=1)


def bc(x):
    return jnp.broadcast_to(x, (8, 128))


def leaf(d, pause):
    sub = lax.broadcasted_iota(jnp.int32, (8, 128), 0)
    lane = lax.broadcasted_iota(jnp.int32, (8, 128), 1)
    d = list(d)
    inv = [(lane == sub + 8 * q).astype(F32) for q in range(16)]
    upper, lower_inv = [], []
    for q in range(16):
        cb = [bc(d[q][:, 8 * q + j : 8 * q + j + 1]) for j in range(8)]
        mul = [[bc(d[p][:, 8 * q + j : 8 * q + j + 1]) for j in range(8)] for p in range(q + 1, 16)]
        zd, zi = d[q], inv[q]
        ud = jnp.zeros((8, 128), F32)
        ui = ud
        for j in range(8):
            pivot = bc(cb[j][j : j + 1, :])
            r = 1.0 / pivot
            rs = lax.rsqrt(pivot)
            rd, ri = bc(zd[j : j + 1, :]), bc(zi[j : j + 1, :])
            mine = sub == j
            ud, ui = jnp.where(mine, rd * rs, ud), jnp.where(mine, ri * rs, ui)
            pd, pi = rd * r, ri * r
            zd = jnp.where(mine, pd, zd - cb[j] * pd)
            zi = jnp.where(mine, pi, zi - cb[j] * pi)
            for k in range(j + 1, 8):
                t = bc(cb[k][j : j + 1, :]) * r
                cb[k] = jnp.where(mine, t, cb[k] - cb[j] * t)
        upper.append(jnp.where(lane >= sub + 8 * q, ud, 0.0))
        lower_inv.append(ui)
        zds = [bc(zd[j : j + 1, :]) for j in range(8)]
        zis = [bc(zi[j : j + 1, :]) for j in range(8)]
        for p in range(q + 1, 16):
            m = mul[p - q - 1]
            x, y = d[p], inv[p]
            for j in range(8):
                x, y = x - m[j] * zds[j], y - m[j] * zis[j]
            d[p], inv[p] = x, y
        if q in (3, 7, 11):
            pause()
    return upper, lower_inv


def factor_block(b, w, u, li, pause):
    s, e = 128 * b, 128 * b + 128
    upper, lower_inv = leaf([w[s + 8 * q : s + 8 * q + 8, s:e] for q in range(16)], pause)
    for q in range(16):
        u[s + 8 * q : s + 8 * q + 8, s:e] = upper[q]
        li[s + 8 * q : s + 8 * q + 8, s:e] = lower_inv[q]
    lb = li[s:e, s:e]
    if b < 3:
        u[s:e, e:] = dotg(lb, w[s:e, e:], 1, 0)
    if b > 0:
        li[s:e, :s] = dotg(lb, li[s:e, :s], 1, 0)
    if b < 3:
        ut = u[s:e, e:]
        w[e:, e:] -= dotg(ut, ut, 0, 0)
        li[e:, :e] -= dotg(ut, li[s:e, :e], 0, 0)


NAMES = ["pc_s", "p0_s", "a0_s", "fr_s", "g_rs", "b0_s", "f0_s", "r_rs"]
NAMES += ["r_b", "bq_w", "bz", "br_g", "br_w", "fr_g", "fr_w"]
NAMES += [(item, step) for item in ("pc", "bc", "a0", "rs") for step in range(4)]
NAMES += [(item, step) for item in range(5) for step in range(5)]
SEM = {name: i for i, name in enumerate(NAMES)}


def main_kernel(
    nx, a_in, p_in, nu, li, m, s, ut, u, pc,
    a, p, load, cm, bct, a0c, br, fr, gp, bp, grs, rb1, rb2, rb3, rb4, rp, rrs, bq, bsw, bsum, bz, w, up, send, recv,
):
    n = nx * nx
    zc, part = n // 2, nx - 1
    r, c = lax.axis_index("row"), lax.axis_index("col")
    y, x = lax.div(r, nx), lax.rem(r, nx)
    z, k = lax.div(c, 2), lax.rem(c, 2)
    partner = c + 1 - 2 * k

    def copy(src, dst, name, axis, index):
        pltpu.make_async_remote_copy(
            src_ref=src, dst_ref=dst, send_sem=send.at[SEM[name]], recv_sem=recv.at[SEM[name]],
            device_id={axis: index}, device_id_type=MESH,
        ).start()

    def wait(ref, name, sems=recv):
        pltpu.make_async_copy(ref, ref, sems.at[SEM[name]]).wait()

    rows = [lax.rem(r + j, n) for j in range(1, n)]
    cols = [lax.rem(c + j, n) for j in range(1, n)]
    cores = [lax.rem(c + 2 * j, n) for j in range(1, zc)]
    def near(v, way):
        one = v + 1 - 2 * lax.rem(v, 2)
        two = lax.rem(v - 1 + 2 * lax.rem(v, 2) + nx, nx)
        return jnp.where(way == 0, one, two)

    def line(zz):
        return lax.div(2 * zz, nx), pl.ds(lax.rem(2 * zz, nx), 2)

    own_line = line(z)

    loads = [pltpu.make_async_copy(p_in, p, load.at[0]), pltpu.make_async_copy(a_in, a, load.at[1])]
    for piece in loads:
        piece.start()
    barrier = pltpu.get_barrier_semaphore()
    for i in rows:
        pl.semaphore_signal(barrier, inc=1, device_id={"row": i}, device_id_type=MESH)
    for i in cols:
        pl.semaphore_signal(barrier, inc=1, device_id={"col": i}, device_id_type=MESH)

    every = slice(None)
    steps = 4 if nx == 4 else 2

    def plan(first, way):
        ya, xa = near(y, way), near(x, way)
        yb, xb = near(y, 1 - way), near(x, 1 - way)
        along_x, along_y = [([(y, x)], y * nx + xa)], [([(y, x)], ya * nx + x)]
        if nx == 4:
            along_x.append(([(y, x), (y, xa)], y * nx + xb))
            along_y.append(([(y, x), (ya, x)], yb * nx + x))
        if first == 0:
            along_x.append(([(y, every)], ya * nx + x))
            if nx == 4:
                along_x.append(([(y, every), (ya, every)], yb * nx + x))
            return along_x
        along_y.append(([(every, x)], y * nx + xa))
        if nx == 4:
            along_y.append(([(every, x), (every, xa)], y * nx + xb))
        return along_y

    full_parts = [((kk, h), plan(h, kk)) for kk in range(2) for h in range(2)]
    half_parts = [(h, plan(h, k)) for h in range(2)]

    def full_got(ref, step):
        return (ref.at[:, 0, 0], ref.at[:, 0, pl.ds(0, 2)], ref.at[:, 0], ref.at[:, pl.ds(0, 2)])[
            step if nx == 4 else 2 * step
        ]

    def half_got(it, step):
        ref = cm.at[it, k]
        return (ref.at[0, 0], ref.at[0, pl.ds(0, 2)], ref.at[0], ref.at[pl.ds(0, 2)])[
            step if nx == 4 else 2 * step
        ]

    def full(ref, item, step):
        if step > steps:
            return
        if step > 0:
            wait(full_got(ref, step - 1), (item, step - 1))
        if step == steps:
            return
        for (kk, h), moves in full_parts:
            pieces, target = moves[step]
            for v, u_ in pieces:
                copy(ref.at[kk, v, u_, h], ref.at[kk, v, u_, h], (item, step), "row", target)

    def half(it, step):
        if step > steps:
            return
        if step > 0:
            wait(half_got(it, step - 1), (it, step - 1))
        if step == steps:
            copy(cm.at[it, k], cm.at[it, k], (it, 4), "col", partner)
            return
        for h, moves in half_parts:
            pieces, target = moves[step]
            for v, u_ in pieces:
                copy(cm.at[it, k, v, u_, h], cm.at[it, k, v, u_, h], (it, step), "row", target)

    def half_end(it):
        wait(cm.at[it, 1 - k], (it, 4))

    halves = (rb1, rb2, rb3, rb4)

    def reduce_step(step):
        if nx == 2 and step in (0, 2):
            return
        for kk in range(2):
            for h in range(2):
                at = 2 * kk + h
                on_y = (h == 0) == (step < 2)
                v = y if on_y else x
                near_a, near_b = near(v, kk), near(v, 1 - kk)
                goal = near_b if step % 2 == 0 else near_a
                target = goal * nx + x if on_y else y * nx + goal
                taken = [goal, near(goal, kk)] if step % 2 == 0 else [goal]
                for j, index in enumerate(taken):
                    other = every if step < 2 else (x if on_y else y)
                    src = bp.at[kk, index, other, h] if on_y else bp.at[kk, other, index, h]
                    dst = halves[step].at[at, j] if step % 2 == 0 else halves[step].at[at]
                    copy(src, dst, ("rs", step), "row", target)

    def reduce_add(step):
        if nx == 2 and step in (0, 2):
            return
        wait(halves[step], ("rs", step))
        for kk in range(2):
            for h in range(2):
                at = 2 * kk + h
                on_y = (h == 0) == (step < 2)
                v = y if on_y else x
                kept = [v, near(v, kk)] if step % 2 == 0 else [v]
                for j, index in enumerate(kept):
                    other = every if step < 2 else (x if on_y else y)
                    got = halves[step][at, j] if step % 2 == 0 else halves[step][at]
                    where_ = (kk, index, other, h) if on_y else (kk, other, index, h)
                    bp[where_] += got

    def whole(ref):
        return ref[...].reshape(512, 512)

    loads[0].wait()
    panel = whole(p)
    mine = pl.ds(pl.multiple_of(k * 256, 256), 256)
    w[...] = panel
    gp[...] = dotg(w[:, mine], panel, 0, 0).reshape(gp.shape)
    loads[1].wait()
    bp[...] = dot3(panel, whole(a), 0, 0).reshape(bp.shape)
    pl.semaphore_wait(barrier, 2 * n - 2)
    for i in rows:
        copy(gp.at[lax.div(i, nx), lax.rem(i, nx)], grs.at[r], "g_rs", "row", i)
    grs[r] = gp[y, x]

    @pl.when(r == c)
    def _():
        for i in rows:
            v, h = lax.div(i, nx), lax.rem(i, nx)
            copy(p.at[:, v, h], pc.at[:, v, h], "pc_s", "row", i)
        pc[:, y, x] = p[:, y, x]

    @pl.when(c == 0)
    def _():
        for j in cols:
            kk, (v, h) = lax.rem(j, 2), line(lax.div(j, 2))
            copy(a.at[kk, v, h], fr.at[kk, v, h], "fr_s", "col", j)
        fr[(k, *own_line)] = a[(k, *own_line)]

    reduce_step(0 if nx == 4 else 1)

    wait(grs.at[pl.ds(0, n - 1)], "g_rs")
    cm[G, k, y, x] = jnp.sum(grs[...], axis=0)
    where = [(h + 2 * q * max(1, zc // 4), h, q) for h in range(2) for q in range(2)]
    reducer = functools.reduce(jnp.logical_or, [c == dst for dst, *_ in where])

    def b_step(step):
        def run():
            if nx == 2 and step == 2:
                reduce_add(1)
                reduce_step(3)
            elif nx == 4:
                reduce_add(step - 1)
                reduce_step(step)
        return run

    def b_done():
        reduce_add(3)
        bct[:, y, x] = bp[:, y, x]
        full(bct, "bc", 0)

        @pl.when(c == 0)
        def _():
            for j in cols:
                kk = lax.rem(j, 2)
                copy(bct.at[kk, y, x], cm.at[B0, kk, y, x], "b0_s", "col", j)
            cm[B0, k, y, x] = bct[k, y, x]

    def pc_start():
        @pl.when(r != c)
        def _():
            wait(pc.at[:, y, x], "pc_s")

        full(pc, "pc", 0)

    def a0_start():
        @pl.when(r != 0)
        def _():
            wait(a0c.at[:, y, x], "a0_s")

        full(a0c, "a0", 0)

        @pl.when(c == 0)
        def _():
            for j in cols:
                kk = lax.rem(j, 2)
                copy(a0c.at[kk, y, x], cm.at[F0, kk, y, x], "f0_s", "col", j)
            cm[F0, k, y, x] = a0c[k, y, x]

    def p0_start():
        @pl.when(r != 0)
        def _():
            wait(cm.at[P0, k, y, x], "p0_s")

        half(P0, 0)

    def fr_start():
        @pl.when(c != 0)
        def _():
            wait(fr.at[(k, *own_line)], "fr_s")

        for j in cores:
            copy(fr.at[(k, *own_line)], fr.at[(k, *own_line)], "fr_g", "col", j)

    def fr_swap():
        wait(bz.at[pl.ds(0, zc - 1)], "fr_g")
        copy(fr.at[k], fr.at[k], "fr_w", "col", partner)

    def bq_start():
        full(pc, "pc", steps)
        bq[...] = dot3(whole(a), whole(pc), 1, 0).reshape(bq.shape)
        copy(bq.at[1 - k], bsw, "bq_w", "col", partner)

    def rp_start():
        rp[...] = dot3(bct[:, y, x].reshape(512 // n, 512), whole(pc), 1, 0).reshape(rp.shape)
        for dst, h, q in where:
            @pl.when(c != dst)
            def _():
                copy(rp.at[h, q], rrs.at[c], "r_rs", "col", dst)

            @pl.when(c == dst)
            def _():
                rrs[c] = rp[h, q]

    def br_reduce():
        wait(bsw, "bq_w")
        bsum[...] = bq[k] + bsw[...]
        for j in cores:
            copy(bsum.at[line(lax.div(j, 2))], bz.at[z], "bz", "col", j)
        bz[z] = bsum[own_line]

    def br_start():
        wait(bz.at[pl.ds(0, zc - 1)], "bz")
        br[(k, *own_line)] = jnp.sum(bz[...], axis=0)
        for j in cores:
            copy(br.at[(k, *own_line)], br.at[(k, *own_line)], "br_g", "col", j)

    def br_swap():
        wait(bz.at[pl.ds(0, zc - 1)], "br_g")
        copy(br.at[k], br.at[k], "br_w", "col", partner)

    def r_reduce():
        for dst, h, q in where:
            @pl.when(c == dst)
            def _():
                wait(rrs.at[pl.ds(0, n - 1)], "r_rs")
                cm[R, h, y, x, q] = jnp.sum(rrs[...], axis=0)
                for j in cores:
                    copy(cm.at[R, h, y, x, q], cm.at[R, h, y, x, q], "r_b", "col", j)

    def r_start():
        @pl.when(reducer)
        def _():
            wait(rrs.at[0], "r_b")

        @pl.when(jnp.logical_not(reducer))
        def _():
            wait(rrs.at[pl.ds(0, 2)], "r_b")

        half(R, 0)

    def b0_start():
        @pl.when(c != 0)
        def _():
            wait(cm.at[B0, k, y, x], "b0_s")

        half(B0, 0)

    def f0_start():
        @pl.when(c != 0)
        def _():
            wait(cm.at[F0, k, y, x], "f0_s")

        half(F0, 0)

    def f(ref, item, step):
        return lambda: full(ref, item, step) if step < steps else None

    def g(it, step):
        return lambda: half(it, step)

    def spread_p0():
        @pl.when(r == 0)
        def _():
            for i in rows:
                v, h = lax.div(i, nx), lax.rem(i, nx)
                copy(p.at[k, v, h], cm.at[P0, k, v, h], "p0_s", "row", i)
            cm[P0, k, y, x] = p[k, y, x]

    def spread_a0(part):
        def run():
            @pl.when(r == 0)
            def _():
                for i in rows[part::5]:
                    v, h = lax.div(i, nx), lax.rem(i, nx)
                    copy(a.at[:, v, h], a0c.at[:, v, h], "a0_s", "row", i)
                if part == 0:
                    a0c[:, y, x] = a[:, y, x]
        return run

    before = [
        g(G, 0), pc_start, spread_a0(0), g(G, 1), b_step(1), fr_start, spread_a0(1),
        g(G, 2), f(pc, "pc", 1), b_step(2), spread_a0(2), g(G, 3), f(pc, "pc", 2), b_step(3),
        spread_a0(3), g(G, 4), f(pc, "pc", 3), b_done, spread_a0(4), spread_p0,
    ]
    for action in before:
        action()

    hooks = [
        [],
        [bq_start],
        [rp_start, f(bct, "bc", 1), a0_start],
        [br_reduce, f(bct, "bc", 2), p0_start, b0_start],
        [r_reduce, f(a0c, "a0", 1)],
        [f(bct, "bc", 3), g(P0, 1), g(B0, 1)],
        [f(a0c, "a0", 2), f0_start],
        [g(P0, 2), g(B0, 2)],
        [r_start, f(a0c, "a0", 3), g(F0, 1)],
        [g(P0, 3), g(B0, 3), br_start],
        [g(F0, 2), g(R, 1)],
        [g(P0, 4), g(B0, 4), g(R, 2)],
        [g(F0, 3), fr_swap],
        [g(R, 3)],
        [g(F0, 4)],
        [g(R, 4)],
    ]

    left = list(hooks)

    def pause():
        for action in left.pop(0):
            action()

    half_end(G)
    w[...] = cm[G].reshape(512, 512)
    up[...] = jnp.zeros((512, 512), F32)
    li[...] = jnp.zeros((512, 512), F32)
    for b in range(4):
        factor_block(b, w, up, li, pause)
        pause()
    nu[...] = -up[...]

    eye = (
        lax.broadcasted_iota(jnp.int32, (512, 512), 0)
        == lax.broadcasted_iota(jnp.int32, (512, 512), 1)
    ).astype(F32)
    lis = split(li[:256, :256]), split(li[256:, :])
    half_end(P0)
    m[...] = eye + lower_times(lis, cm[P0].reshape(512, 512), 1)
    full(a0c, "a0", steps)
    full(bct, "bc", steps)
    ut[...] = lower_times(lis, whole(bct), 0) + whole(a0c)
    br_swap()
    half_end(B0)
    half_end(F0)
    s[...] = lower_times(lis, cm[B0].reshape(512, 512), 0)
    s[...] += s[...].T + cm[F0].reshape(512, 512)
    half_end(R)
    s[...] += lower_times(lis, times_upper(cm[R].reshape(512, 512), lis), 0)
    wait(br.at[1 - k], "br_w")
    wait(fr.at[1 - k], "fr_w")
    u[...] = times_upper(whole(br), lis) + whole(fr)

    scattered = grs.at[pl.ds(0, n - 1)]

    slices = cm.at[:, :, 0, pl.ds(0, 3)] if nx == 4 else cm.at[pl.ds(0, 3), :, 0, 0]

    def wait_slices(name, sems):
        wait(slices, name, sems)

    @pl.when(r == c)
    def _():
        wait_slices( "pc_s", send)

    @pl.when(r == 0)
    def _():
        wait(scattered, "p0_s", send)
        wait_slices( "a0_s", send)

    @pl.when(c == 0)
    def _():
        wait_slices( "fr_s", send)
        wait(scattered, "b0_s", send)
        wait(scattered, "f0_s", send)

    wait(scattered, "g_rs", send)
    for step in range(steps):
        for item in ("pc", "bc", "a0"):
            wait(full_got(pc, step), (item, step), send)
        for it in range(5):
            wait(half_got(it, step), (it, step), send)
    for step in range(4):
        if nx == 4 or step in (1, 3):
            wait(halves[step], ("rs", step), send)
    for name in ("bq_w", "br_w", "fr_w", *((it, 4) for it in range(5))):
        wait(cm.at[0, 0], name, send)
    for name in ("bz", "br_g", "fr_g"):
        wait(bz.at[pl.ds(0, zc - 1)], name, send)

    @pl.when(reducer)
    def _():
        wait(rrs.at[pl.ds(0, 3)], "r_rs", send)
        wait(rrs.at[pl.ds(0, zc - 1)], "r_b", send)

    @pl.when(jnp.logical_not(reducer))
    def _():
        wait(rrs.at[pl.ds(0, 4)], "r_rs", send)


def final_kernel(a, p, nu, li, m, s, ut, u, pc, out, band, xx, e, save):
    top = pltpu.make_async_copy(nu, band, save.at[4])
    top.start()
    r, c = lax.axis_index("row"), lax.axis_index("col")
    eye = (
        lax.broadcasted_iota(jnp.int32, (512, 512), 0)
        == lax.broadcasted_iota(jnp.int32, (512, 512), 1)
    ).astype(F32)
    start = 0.9
    e[...] = eye - start * m[...]
    xx[...] = start * (eye + e[...])

    def more(state):
        step, now = state
        return jnp.logical_and(step < 48, now > 0.1)

    def square(state):
        step, _ = state
        es = split(e[...])
        ee = dot3(es, es, 1, 0)
        e[...] = ee
        xx[...] += dot3(xx[...], ee, 1, 0)
        return step + 1, jnp.sum(ee * ee)

    lax.while_loop(more, square, (jnp.int32(0), jnp.float32(1.0)))

    ms = split(m[...])

    def rough(state):
        step, now = state
        return jnp.logical_and(step < 5, now > 1e-5)

    def newton(state):
        step, _ = state
        xs = split(xx[...])
        rest = eye - dot3(ms, xs, 1, 0)
        xx[...] += dot3(xs, rest, 1, 0)
        return step + 1, jnp.sum(rest * rest)

    lax.while_loop(rough, newton, (jnp.int32(0), jnp.float32(1.0)))
    xs = split(xx[...])
    tail = tuple(v[:, 256:] for v in xs)
    nis = split(jnp.concatenate(
        [dot3(xs, li[:, :256], 1, 0), dot3(tail, li[256:, 256:], 1, 0)], axis=1
    ))
    yts = split(jnp.where(c == 0, eye, dot3(nis, pc[...], 1, 1)))
    zts = split(ut[...] - dot3(s[...], yts, 1, 0))
    xx[...] = jnp.where(r == 0, eye, dot3(p[...], nis, 1, 1))
    saves = []
    for q in range(4):
        part = pl.ds(128 * q, 128)
        e[part] = a[part] - dot3(xx[part], zts, 1, 0) - dot3(u[part], yts, 1, 0)
        saves.append(pltpu.make_async_copy(e.at[part], out.at[part], save.at[q]))
        saves[-1].start()
    for copy in [top, *saves]:
        copy.wait()


def solution(mesh):
    n = mesh.shape["row"]
    nx = {4: 2, 16: 4}[n]
    zc, rr = n // 2, 128 // n
    vm = pl.BlockSpec(memory_space=pltpu.VMEM)
    hbm = pl.BlockSpec(memory_space=pltpu.HBM)
    sq = jax.ShapeDtypeStruct((512, 512), F32)
    shape = (2, nx, nx, 2, rr, 512)

    def scratch(*lead):
        return pltpu.VMEM((*lead, 512), F32)

    def step(trailing, panel):
        nu, li, m, s, ut, u, pc = pl.pallas_call(
            functools.partial(main_kernel, nx),
            out_shape=[sq] * 6 + [jax.ShapeDtypeStruct(shape, F32)],
            in_specs=[hbm] * 2,
            out_specs=[vm] * 7,
            scratch_shapes=[
                scratch(*shape[:-1]),
                scratch(*shape[:-1]),
                pltpu.SemaphoreType.DMA((2,)),
                scratch(5, *shape[:-1]),
                scratch(*shape[:-1]),
                scratch(*shape[:-1]),
                scratch(*shape[:-1]),
                scratch(*shape[:-1]),
                scratch(*shape[1:-1]),
                scratch(*shape[:-1]),
                scratch(n, 2, rr),
                scratch(4, 2, nx, rr),
                scratch(4, nx, rr),
                scratch(4, 2, rr),
                scratch(4, rr),
                scratch(2, 2, rr),
                scratch(n, rr),
                scratch(*shape[:-1]),
                scratch(*shape[1:-1]),
                scratch(*shape[1:-1]),
                scratch(zc, 2, 2, rr),
                scratch(512),
                scratch(512),
                pltpu.SemaphoreType.DMA((len(NAMES),)),
                pltpu.SemaphoreType.DMA((len(NAMES),)),
            ],
            compiler_params=pltpu.CompilerParams(collective_id=0, has_side_effects=True, vmem_limit_bytes=34 << 20),
            name="exchange_factor",
        )(
            pltpu.with_memory_space_constraint(trailing.reshape(shape), pltpu.HBM),
            pltpu.with_memory_space_constraint(panel.reshape(shape), pltpu.HBM),
        )
        return pl.pallas_call(
            final_kernel,
            out_shape=[sq, sq],
            in_specs=[vm] * 9,
            out_specs=[hbm] * 2,
            scratch_shapes=[pltpu.VMEM((512, 512), F32)] * 2 + [pltpu.SemaphoreType.DMA((5,))],
            compiler_params=pltpu.CompilerParams(vmem_limit_bytes=30 << 20),
            name="update",
        )(trailing, panel, nu, li, m, s, ut, u, pc.reshape(512, 512))

    return jax.shard_map(
        step, mesh=mesh, in_specs=(P("row", "col"), P("row", None)),
        out_specs=(P("row", "col"), P()), check_vma=False,
    )
```

```python
import functools
import jax
import jax.numpy as jnp
from jax import lax
from jax.experimental import pallas as pl
from jax.experimental.pallas import tpu as pltpu
from jax.sharding import PartitionSpec as P

HI = lax.Precision.HIGHEST
F32 = jnp.float32
BF16 = jnp.bfloat16
MESH = pl.DeviceIdType.MESH
G, P0, B0, F0, R = range(5)


def dotg(a, b, ca, cb):
    return lax.dot_general(
        a, b, (((ca,), (cb,)), ((), ())), precision=HI, preferred_element_type=F32
    )


def split(x):
    high = x.astype(BF16)
    return high, (x - high.astype(F32)).astype(BF16)


def dot3(a, b, ca, cb):
    ah, al = a if isinstance(a, tuple) else split(a)
    bh, bl = b if isinstance(b, tuple) else split(b)
    dims = (((ca,), (cb,)), ((), ()))
    d = functools.partial(lax.dot_general, dimension_numbers=dims, preferred_element_type=F32)
    return d(ah, bh) + (d(ah, bl) + d(al, bh))


def lower_times(lower, x, cb):
    xs = split(x)
    head = tuple(v[:256] if cb == 0 else v[:, :256] for v in xs)
    return jnp.concatenate([dot3(lower[0], head, 1, cb), dot3(lower[1], xs, 1, cb)], axis=0)


def times_upper(x, lower):
    xs = split(x)
    head = tuple(v[:, :256] for v in xs)
    return jnp.concatenate([dot3(head, lower[0], 1, 1), dot3(xs, lower[1], 1, 1)], axis=1)


def bc(x):
    return jnp.broadcast_to(x, (8, 128))


def leaf(d, pause):
    sub = lax.broadcasted_iota(jnp.int32, (8, 128), 0)
    lane = lax.broadcasted_iota(jnp.int32, (8, 128), 1)
    d = list(d)
    inv = [(lane == sub + 8 * q).astype(F32) for q in range(16)]
    upper, lower_inv = [], []
    for q in range(16):
        cb = [bc(d[q][:, 8 * q + j : 8 * q + j + 1]) for j in range(8)]
        mul = [[bc(d[p][:, 8 * q + j : 8 * q + j + 1]) for j in range(8)] for p in range(q + 1, 16)]
        zd, zi = d[q], inv[q]
        ud = jnp.zeros((8, 128), F32)
        ui = ud
        for j in range(8):
            pivot = bc(cb[j][j : j + 1, :])
            r = 1.0 / pivot
            rs = lax.rsqrt(pivot)
            rd, ri = bc(zd[j : j + 1, :]), bc(zi[j : j + 1, :])
            mine = sub == j
            ud, ui = jnp.where(mine, rd * rs, ud), jnp.where(mine, ri * rs, ui)
            pd, pi = rd * r, ri * r
            zd = jnp.where(mine, pd, zd - cb[j] * pd)
            zi = jnp.where(mine, pi, zi - cb[j] * pi)
            for k in range(j + 1, 8):
                t = bc(cb[k][j : j + 1, :]) * r
                cb[k] = jnp.where(mine, t, cb[k] - cb[j] * t)
        upper.append(jnp.where(lane >= sub + 8 * q, ud, 0.0))
        lower_inv.append(ui)
        zds = [bc(zd[j : j + 1, :]) for j in range(8)]
        zis = [bc(zi[j : j + 1, :]) for j in range(8)]
        for p in range(q + 1, 16):
            m = mul[p - q - 1]
            x, y = d[p], inv[p]
            for j in range(8):
                x, y = x - m[j] * zds[j], y - m[j] * zis[j]
            d[p], inv[p] = x, y
        if q in (3, 7, 11):
            pause()
    return upper, lower_inv


def factor_block(b, w, u, li, pause):
    s, e = 128 * b, 128 * b + 128
    upper, lower_inv = leaf([w[s + 8 * q : s + 8 * q + 8, s:e] for q in range(16)], pause)
    for q in range(16):
        u[s + 8 * q : s + 8 * q + 8, s:e] = upper[q]
        li[s + 8 * q : s + 8 * q + 8, s:e] = lower_inv[q]
    lb = li[s:e, s:e]
    if b < 3:
        u[s:e, e:] = dotg(lb, w[s:e, e:], 1, 0)
    if b > 0:
        li[s:e, :s] = dotg(lb, li[s:e, :s], 1, 0)
    if b < 3:
        ut = u[s:e, e:]
        w[e:, e:] -= dotg(ut, ut, 0, 0)
        li[e:, :e] -= dotg(ut, li[s:e, :e], 0, 0)


NAMES = ["pc_s", "p0_s", "a0_s", "fr_s", "g_rs", "b0_s", "f0_s", "r_rs"]
NAMES += ["r_b", "bq_w", "bz", "br_g", "br_w", "fr_g", "fr_w"]
NAMES += [(item, step) for item in ("pc", "bc", "a0", "rs") for step in range(4)]
NAMES += [(item, step) for item in range(5) for step in range(5)]
SEM = {name: i for i, name in enumerate(NAMES)}


def main_kernel(
    nx, a_in, p_in, nu, li, m, s, ut, u, pc,
    a, p, load, cm, bct, a0c, br, fr, gp, bp, grs, rb1, rb2, rb3, rb4, rp, rrs, bq, bsw, bsum, bz, w, up, send, recv,
):
    n = nx * nx
    zc, part = n // 2, nx - 1
    r, c = lax.axis_index("row"), lax.axis_index("col")
    y, x = lax.div(r, nx), lax.rem(r, nx)
    z, k = lax.div(c, 2), lax.rem(c, 2)
    partner = c + 1 - 2 * k

    def copy(src, dst, name, axis, index):
        pltpu.make_async_remote_copy(
            src_ref=src, dst_ref=dst, send_sem=send.at[SEM[name]], recv_sem=recv.at[SEM[name]],
            device_id={axis: index}, device_id_type=MESH,
        ).start()

    def wait(ref, name, sems=recv):
        pltpu.make_async_copy(ref, ref, sems.at[SEM[name]]).wait()

    rows = [lax.rem(r + j, n) for j in range(1, n)]
    cols = [lax.rem(c + j, n) for j in range(1, n)]
    cores = [lax.rem(c + 2 * j, n) for j in range(1, zc)]
    def near(v, way):
        one = v + 1 - 2 * lax.rem(v, 2)
        two = lax.rem(v - 1 + 2 * lax.rem(v, 2) + nx, nx)
        return jnp.where(way == 0, one, two)

    def line(zz):
        return lax.div(2 * zz, nx), pl.ds(lax.rem(2 * zz, nx), 2)

    own_line = line(z)

    loads = [pltpu.make_async_copy(p_in, p, load.at[0]), pltpu.make_async_copy(a_in, a, load.at[1])]
    for piece in loads:
        piece.start()
    barrier = pltpu.get_barrier_semaphore()
    for i in rows:
        pl.semaphore_signal(barrier, inc=1, device_id={"row": i}, device_id_type=MESH)
    for i in cols:
        pl.semaphore_signal(barrier, inc=1, device_id={"col": i}, device_id_type=MESH)

    every = slice(None)
    steps = 4 if nx == 4 else 2

    def plan(first, way):
        ya, xa = near(y, way), near(x, way)
        yb, xb = near(y, 1 - way), near(x, 1 - way)
        along_x, along_y = [([(y, x)], y * nx + xa)], [([(y, x)], ya * nx + x)]
        if nx == 4:
            along_x.append(([(y, x), (y, xa)], y * nx + xb))
            along_y.append(([(y, x), (ya, x)], yb * nx + x))
        if first == 0:
            along_x.append(([(y, every)], ya * nx + x))
            if nx == 4:
                along_x.append(([(y, every), (ya, every)], yb * nx + x))
            return along_x
        along_y.append(([(every, x)], y * nx + xa))
        if nx == 4:
            along_y.append(([(every, x), (every, xa)], y * nx + xb))
        return along_y

    full_parts = [((kk, h), plan(h, kk)) for kk in range(2) for h in range(2)]
    half_parts = [(h, plan(h, k)) for h in range(2)]

    def full_got(ref, step):
        return (ref.at[:, 0, 0], ref.at[:, 0, pl.ds(0, 2)], ref.at[:, 0], ref.at[:, pl.ds(0, 2)])[
            step if nx == 4 else 2 * step
        ]

    def half_got(it, step):
        ref = cm.at[it, k]
        return (ref.at[0, 0], ref.at[0, pl.ds(0, 2)], ref.at[0], ref.at[pl.ds(0, 2)])[
            step if nx == 4 else 2 * step
        ]

    def full(ref, item, step):
        if step > steps:
            return
        if step > 0:
            wait(full_got(ref, step - 1), (item, step - 1))
        if step == steps:
            return
        for (kk, h), moves in full_parts:
            pieces, target = moves[step]
            for v, u_ in pieces:
                copy(ref.at[kk, v, u_, h], ref.at[kk, v, u_, h], (item, step), "row", target)

    def half(it, step):
        if step > steps:
            return
        if step > 0:
            wait(half_got(it, step - 1), (it, step - 1))
        if step == steps:
            copy(cm.at[it, k], cm.at[it, k], (it, 4), "col", partner)
            return
        for h, moves in half_parts:
            pieces, target = moves[step]
            for v, u_ in pieces:
                copy(cm.at[it, k, v, u_, h], cm.at[it, k, v, u_, h], (it, step), "row", target)

    def half_end(it):
        wait(cm.at[it, 1 - k], (it, 4))

    halves = (rb1, rb2, rb3, rb4)

    def reduce_step(step):
        if nx == 2 and step in (0, 2):
            return
        for kk in range(2):
            for h in range(2):
                at = 2 * kk + h
                on_y = (h == 0) == (step < 2)
                v = y if on_y else x
                near_a, near_b = near(v, kk), near(v, 1 - kk)
                goal = near_b if step % 2 == 0 else near_a
                target = goal * nx + x if on_y else y * nx + goal
                taken = [goal, near(goal, kk)] if step % 2 == 0 else [goal]
                for j, index in enumerate(taken):
                    other = every if step < 2 else (x if on_y else y)
                    src = bp.at[kk, index, other, h] if on_y else bp.at[kk, other, index, h]
                    dst = halves[step].at[at, j] if step % 2 == 0 else halves[step].at[at]
                    copy(src, dst, ("rs", step), "row", target)

    def reduce_add(step):
        if nx == 2 and step in (0, 2):
            return
        wait(halves[step], ("rs", step))
        for kk in range(2):
            for h in range(2):
                at = 2 * kk + h
                on_y = (h == 0) == (step < 2)
                v = y if on_y else x
                kept = [v, near(v, kk)] if step % 2 == 0 else [v]
                for j, index in enumerate(kept):
                    other = every if step < 2 else (x if on_y else y)
                    got = halves[step][at, j] if step % 2 == 0 else halves[step][at]
                    where_ = (kk, index, other, h) if on_y else (kk, other, index, h)
                    bp[where_] += got

    def whole(ref):
        return ref[...].reshape(512, 512)

    loads[0].wait()
    panel = whole(p)
    mine = pl.ds(pl.multiple_of(k * 256, 256), 256)
    w[...] = panel
    gp[...] = dotg(w[:, mine], panel, 0, 0).reshape(gp.shape)
    loads[1].wait()
    bp[...] = dot3(panel, whole(a), 0, 0).reshape(bp.shape)
    pl.semaphore_wait(barrier, 2 * n - 2)
    for i in rows:
        copy(gp.at[lax.div(i, nx), lax.rem(i, nx)], grs.at[r], "g_rs", "row", i)
    grs[r] = gp[y, x]

    @pl.when(r == c)
    def _():
        for i in rows:
            v, h = lax.div(i, nx), lax.rem(i, nx)
            copy(p.at[:, v, h], pc.at[:, v, h], "pc_s", "row", i)
        pc[:, y, x] = p[:, y, x]

    @pl.when(c == 0)
    def _():
        for j in cols:
            kk, (v, h) = lax.rem(j, 2), line(lax.div(j, 2))
            copy(a.at[kk, v, h], fr.at[kk, v, h], "fr_s", "col", j)
        fr[(k, *own_line)] = a[(k, *own_line)]

    reduce_step(0 if nx == 4 else 1)

    wait(grs.at[pl.ds(0, n - 1)], "g_rs")
    cm[G, k, y, x] = jnp.sum(grs[...], axis=0)
    where = [(h + 2 * q * max(1, zc // 4), h, q) for h in range(2) for q in range(2)]
    reducer = functools.reduce(jnp.logical_or, [c == dst for dst, *_ in where])

    def b_step(step):
        def run():
            if nx == 2 and step == 2:
                reduce_add(1)
                reduce_step(3)
            elif nx == 4:
                reduce_add(step - 1)
                reduce_step(step)
        return run

    def b_done():
        reduce_add(3)
        bct[:, y, x] = bp[:, y, x]
        full(bct, "bc", 0)

        @pl.when(c == 0)
        def _():
            for j in cols:
                kk = lax.rem(j, 2)
                copy(bct.at[kk, y, x], cm.at[B0, kk, y, x], "b0_s", "col", j)
            cm[B0, k, y, x] = bct[k, y, x]

    def pc_start():
        @pl.when(r != c)
        def _():
            wait(pc.at[:, y, x], "pc_s")

        full(pc, "pc", 0)

    def a0_start():
        @pl.when(r != 0)
        def _():
            wait(a0c.at[:, y, x], "a0_s")

        full(a0c, "a0", 0)

        @pl.when(c == 0)
        def _():
            for j in cols:
                kk = lax.rem(j, 2)
                copy(a0c.at[kk, y, x], cm.at[F0, kk, y, x], "f0_s", "col", j)
            cm[F0, k, y, x] = a0c[k, y, x]

    def p0_start():
        @pl.when(r != 0)
        def _():
            wait(cm.at[P0, k, y, x], "p0_s")

        half(P0, 0)

    def fr_start():
        @pl.when(c != 0)
        def _():
            wait(fr.at[(k, *own_line)], "fr_s")

        for j in cores:
            copy(fr.at[(k, *own_line)], fr.at[(k, *own_line)], "fr_g", "col", j)

    def fr_swap():
        wait(bz.at[pl.ds(0, zc - 1)], "fr_g")
        copy(fr.at[k], fr.at[k], "fr_w", "col", partner)

    def bq_start():
        full(pc, "pc", steps)
        bq[...] = dot3(whole(a), whole(pc), 1, 0).reshape(bq.shape)
        copy(bq.at[1 - k], bsw, "bq_w", "col", partner)

    def rp_start():
        rp[...] = dot3(bct[:, y, x].reshape(512 // n, 512), whole(pc), 1, 0).reshape(rp.shape)
        for dst, h, q in where:
            @pl.when(c != dst)
            def _():
                copy(rp.at[h, q], rrs.at[c], "r_rs", "col", dst)

            @pl.when(c == dst)
            def _():
                rrs[c] = rp[h, q]

    def br_reduce():
        wait(bsw, "bq_w")
        bsum[...] = bq[k] + bsw[...]
        for j in cores:
            copy(bsum.at[line(lax.div(j, 2))], bz.at[z], "bz", "col", j)
        bz[z] = bsum[own_line]

    def br_start():
        wait(bz.at[pl.ds(0, zc - 1)], "bz")
        br[(k, *own_line)] = jnp.sum(bz[...], axis=0)
        for j in cores:
            copy(br.at[(k, *own_line)], br.at[(k, *own_line)], "br_g", "col", j)

    def br_swap():
        wait(bz.at[pl.ds(0, zc - 1)], "br_g")
        copy(br.at[k], br.at[k], "br_w", "col", partner)

    def r_reduce():
        for dst, h, q in where:
            @pl.when(c == dst)
            def _():
                wait(rrs.at[pl.ds(0, n - 1)], "r_rs")
                cm[R, h, y, x, q] = jnp.sum(rrs[...], axis=0)
                for j in cores:
                    copy(cm.at[R, h, y, x, q], cm.at[R, h, y, x, q], "r_b", "col", j)

    def r_start():
        @pl.when(reducer)
        def _():
            wait(rrs.at[0], "r_b")

        @pl.when(jnp.logical_not(reducer))
        def _():
            wait(rrs.at[pl.ds(0, 2)], "r_b")

        half(R, 0)

    def b0_start():
        @pl.when(c != 0)
        def _():
            wait(cm.at[B0, k, y, x], "b0_s")

        half(B0, 0)

    def f0_start():
        @pl.when(c != 0)
        def _():
            wait(cm.at[F0, k, y, x], "f0_s")

        half(F0, 0)

    def f(ref, item, step):
        return lambda: full(ref, item, step) if step < steps else None

    def g(it, step):
        return lambda: half(it, step)

    def spread_p0():
        @pl.when(r == 0)
        def _():
            for i in rows:
                v, h = lax.div(i, nx), lax.rem(i, nx)
                copy(p.at[k, v, h], cm.at[P0, k, v, h], "p0_s", "row", i)
            cm[P0, k, y, x] = p[k, y, x]

    def spread_a0(part):
        def run():
            @pl.when(r == 0)
            def _():
                for i in rows[part::5]:
                    v, h = lax.div(i, nx), lax.rem(i, nx)
                    copy(a.at[:, v, h], a0c.at[:, v, h], "a0_s", "row", i)
                if part == 0:
                    a0c[:, y, x] = a[:, y, x]
        return run

    before = [
        g(G, 0), pc_start, spread_a0(0), g(G, 1), b_step(1), fr_start, spread_a0(1),
        g(G, 2), f(pc, "pc", 1), b_step(2), spread_a0(2), g(G, 3), f(pc, "pc", 2), b_step(3),
        g(G, 4), f(pc, "pc", 3), b_done, spread_a0(3),
    ]
    for action in before:
        action()

    hooks = [
        [spread_a0(4), spread_p0],
        [bq_start],
        [rp_start, f(bct, "bc", 1), a0_start],
        [br_reduce, f(bct, "bc", 2), p0_start, b0_start],
        [r_reduce, f(a0c, "a0", 1)],
        [f(bct, "bc", 3), g(P0, 1), g(B0, 1)],
        [f(a0c, "a0", 2), f0_start],
        [g(P0, 2), g(B0, 2)],
        [r_start, f(a0c, "a0", 3), g(F0, 1)],
        [g(P0, 3), g(B0, 3), br_start],
        [g(F0, 2), g(R, 1)],
        [g(P0, 4), g(B0, 4), g(R, 2)],
        [g(F0, 3), fr_swap],
        [g(R, 3)],
        [g(F0, 4)],
        [g(R, 4)],
    ]

    left = list(hooks)

    def pause():
        for action in left.pop(0):
            action()

    half_end(G)
    w[...] = cm[G].reshape(512, 512)
    up[...] = jnp.zeros((512, 512), F32)
    li[...] = jnp.zeros((512, 512), F32)
    for b in range(4):
        factor_block(b, w, up, li, pause)
        pause()
    nu[...] = -up[...]

    eye = (
        lax.broadcasted_iota(jnp.int32, (512, 512), 0)
        == lax.broadcasted_iota(jnp.int32, (512, 512), 1)
    ).astype(F32)
    lis = split(li[:256, :256]), split(li[256:, :])
    half_end(P0)
    m[...] = eye + lower_times(lis, cm[P0].reshape(512, 512), 1)
    full(a0c, "a0", steps)
    full(bct, "bc", steps)
    ut[...] = lower_times(lis, whole(bct), 0) + whole(a0c)
    br_swap()
    half_end(B0)
    half_end(F0)
    s[...] = lower_times(lis, cm[B0].reshape(512, 512), 0)
    s[...] += s[...].T + cm[F0].reshape(512, 512)
    half_end(R)
    s[...] += lower_times(lis, times_upper(cm[R].reshape(512, 512), lis), 0)
    wait(br.at[1 - k], "br_w")
    wait(fr.at[1 - k], "fr_w")
    u[...] = times_upper(whole(br), lis) + whole(fr)

    scattered = grs.at[pl.ds(0, n - 1)]

    slices = cm.at[:, :, 0, pl.ds(0, 3)] if nx == 4 else cm.at[pl.ds(0, 3), :, 0, 0]

    def wait_slices(name, sems):
        wait(slices, name, sems)

    @pl.when(r == c)
    def _():
        wait_slices( "pc_s", send)

    @pl.when(r == 0)
    def _():
        wait(scattered, "p0_s", send)
        wait_slices( "a0_s", send)

    @pl.when(c == 0)
    def _():
        wait_slices( "fr_s", send)
        wait(scattered, "b0_s", send)
        wait(scattered, "f0_s", send)

    wait(scattered, "g_rs", send)
    for step in range(steps):
        for item in ("pc", "bc", "a0"):
            wait(full_got(pc, step), (item, step), send)
        for it in range(5):
            wait(half_got(it, step), (it, step), send)
    for step in range(4):
        if nx == 4 or step in (1, 3):
            wait(halves[step], ("rs", step), send)
    for name in ("bq_w", "br_w", "fr_w", *((it, 4) for it in range(5))):
        wait(cm.at[0, 0], name, send)
    for name in ("bz", "br_g", "fr_g"):
        wait(bz.at[pl.ds(0, zc - 1)], name, send)

    @pl.when(reducer)
    def _():
        wait(rrs.at[pl.ds(0, 3)], "r_rs", send)
        wait(rrs.at[pl.ds(0, zc - 1)], "r_b", send)

    @pl.when(jnp.logical_not(reducer))
    def _():
        wait(rrs.at[pl.ds(0, 4)], "r_rs", send)


def final_kernel(a, p, nu, li, m, s, ut, u, pc, out, band, xx, e, save):
    top = pltpu.make_async_copy(nu, band, save.at[4])
    top.start()
    r, c = lax.axis_index("row"), lax.axis_index("col")
    eye = (
        lax.broadcasted_iota(jnp.int32, (512, 512), 0)
        == lax.broadcasted_iota(jnp.int32, (512, 512), 1)
    ).astype(F32)
    start = 0.9
    e[...] = eye - start * m[...]
    xx[...] = start * (eye + e[...])

    def more(state):
        step, now = state
        return jnp.logical_and(step < 48, now > 0.1)

    def square(state):
        step, _ = state
        es = split(e[...])
        ee = dot3(es, es, 1, 0)
        e[...] = ee
        xx[...] += dot3(xx[...], ee, 1, 0)
        return step + 1, jnp.sum(ee * ee)

    lax.while_loop(more, square, (jnp.int32(0), jnp.float32(1.0)))

    ms = split(m[...])

    def rough(state):
        step, now = state
        return jnp.logical_and(step < 5, now > 1e-5)

    def newton(state):
        step, _ = state
        xs = split(xx[...])
        rest = eye - dot3(ms, xs, 1, 0)
        xx[...] += dot3(xs, rest, 1, 0)
        return step + 1, jnp.sum(rest * rest)

    lax.while_loop(rough, newton, (jnp.int32(0), jnp.float32(1.0)))
    xs = split(xx[...])
    tail = tuple(v[:, 256:] for v in xs)
    nis = split(jnp.concatenate(
        [dot3(xs, li[:, :256], 1, 0), dot3(tail, li[256:, 256:], 1, 0)], axis=1
    ))
    yts = split(jnp.where(c == 0, eye, dot3(nis, pc[...], 1, 1)))
    zts = split(ut[...] - dot3(s[...], yts, 1, 0))
    xx[...] = jnp.where(r == 0, eye, dot3(p[...], nis, 1, 1))
    saves = []
    for q in range(4):
        part = pl.ds(128 * q, 128)
        e[part] = a[part] - dot3(xx[part], zts, 1, 0) - dot3(u[part], yts, 1, 0)
        saves.append(pltpu.make_async_copy(e.at[part], out.at[part], save.at[q]))
        saves[-1].start()
    for copy in [top, *saves]:
        copy.wait()


def solution(mesh):
    n = mesh.shape["row"]
    nx = {4: 2, 16: 4}[n]
    zc, rr = n // 2, 128 // n
    vm = pl.BlockSpec(memory_space=pltpu.VMEM)
    hbm = pl.BlockSpec(memory_space=pltpu.HBM)
    sq = jax.ShapeDtypeStruct((512, 512), F32)
    shape = (2, nx, nx, 2, rr, 512)

    def scratch(*lead):
        return pltpu.VMEM((*lead, 512), F32)

    def step(trailing, panel):
        nu, li, m, s, ut, u, pc = pl.pallas_call(
            functools.partial(main_kernel, nx),
            out_shape=[sq] * 6 + [jax.ShapeDtypeStruct(shape, F32)],
            in_specs=[hbm] * 2,
            out_specs=[vm] * 7,
            scratch_shapes=[
                scratch(*shape[:-1]),
                scratch(*shape[:-1]),
                pltpu.SemaphoreType.DMA((2,)),
                scratch(5, *shape[:-1]),
                scratch(*shape[:-1]),
                scratch(*shape[:-1]),
                scratch(*shape[:-1]),
                scratch(*shape[:-1]),
                scratch(*shape[1:-1]),
                scratch(*shape[:-1]),
                scratch(n, 2, rr),
                scratch(4, 2, nx, rr),
                scratch(4, nx, rr),
                scratch(4, 2, rr),
                scratch(4, rr),
                scratch(2, 2, rr),
                scratch(n, rr),
                scratch(*shape[:-1]),
                scratch(*shape[1:-1]),
                scratch(*shape[1:-1]),
                scratch(zc, 2, 2, rr),
                scratch(512),
                scratch(512),
                pltpu.SemaphoreType.DMA((len(NAMES),)),
                pltpu.SemaphoreType.DMA((len(NAMES),)),
            ],
            compiler_params=pltpu.CompilerParams(collective_id=0, has_side_effects=True, vmem_limit_bytes=34 << 20),
            name="exchange_factor",
        )(
            pltpu.with_memory_space_constraint(trailing.reshape(shape), pltpu.HBM),
            pltpu.with_memory_space_constraint(panel.reshape(shape), pltpu.HBM),
        )
        return pl.pallas_call(
            final_kernel,
            out_shape=[sq, sq],
            in_specs=[vm] * 9,
            out_specs=[hbm] * 2,
            scratch_shapes=[pltpu.VMEM((512, 512), F32)] * 2 + [pltpu.SemaphoreType.DMA((5,))],
            compiler_params=pltpu.CompilerParams(vmem_limit_bytes=30 << 20),
            name="update",
        )(trailing, panel, nu, li, m, s, ut, u, pc.reshape(512, 512))

    return jax.shard_map(
        step, mesh=mesh, in_specs=(P("row", "col"), P("row", None)),
        out_specs=(P("row", "col"), P()), check_vma=False,
    )
```
